256 devices in a mesh: blk: 32 (over x, z_lo, core), uly: 8 (over y, z_hi).
Axes of the slice: x: 4, y: 4, z: 8 (z_hi: 2, z_lo: 4; z = z_hi * 4 + z_lo), core: 2. Of those that a mesh axis runs over, the one named last changes fastest.
Arguments:
- video_tokens: bfloat16 [12288, 3072], P(('blk', 'uly')), may hold values from -6 to 6
- text_tokens: bfloat16 [256, 3072], P('uly'), may hold values from -6 to 6
- video_modulation: bfloat16 [3, 3072], replicated, may hold values from -4 to 4
- text_modulation: bfloat16 [3, 3072], replicated, may hold values from -4 to 4
- video_projection: bfloat16 [3072, 3, 2048], P(None, None, 'uly'), may hold values from -0.109375 to 0.109375
- text_projection: bfloat16 [3072, 3, 2048], P(None, None, 'uly'), may hold values from -0.109375 to 0.109375
- video_output: bfloat16 [2048, 3072], P('uly'), may hold values from -0.125 to 0.125
- text_output: bfloat16 [2048, 3072], P('uly'), may hold values from -0.125 to 0.125
- video_gains: float32 [2, 128], replicated, may hold values from 1 to 12
- text_gains: float32 [2, 128], replicated, may hold values from 1 to 12
Outputs:
- video_attention: bfloat16 [12288, 3072], P(('blk', 'uly'))
- text_attention: bfloat16 [256, 3072], P('uly')
The draws below stay inside these ranges and needn't reach their ends.
All inputs are finite; a program needn't handle non-finite values.
Results may differ from the reference program's by a relative error of at most 0.025.
The reference program's roundings to bfloat16 on the way count: a program that leaves them out, or rounds other values in their place, can miss the bound.
Values may be sent and summed in bfloat16 or wider, within the bound.
A program may use at most 128 MiB of HBM per device.

```python
import math
import jax
import jax.numpy as jnp
from jax import lax

D = 3072
HD = 128
HEADS = 16
TEXT = 256
VIDEO = 12288
N_ULY = 8


def norm_gains(seed_key):
    baseline_key = jax.random.fold_in(seed_key, 0)
    return jax.random.uniform(baseline_key, (2, HD), jnp.float32, 1.4, 2.6)


def draw_video_gains(key, part):
    return norm_gains(jax.random.fold_in(key, 11))


def draw_text_gains(key, part):
    return norm_gains(jax.random.fold_in(key, 23))


def levels(own_key, extent, cuts, smallest, top_value):
    loudness = 1.0
    for dim, blocks in cuts:
        draws = jax.random.uniform(jax.random.fold_in(jax.random.fold_in(own_key, 6), dim), (blocks,), jnp.float32, smallest / len(cuts), top_value / len(cuts))
        loudness = loudness * jnp.repeat(jnp.exp(draws), extent[dim] // blocks).reshape((-1,) + (1,) * (len(extent) - 1 - dim))
    return loudness


def gaussian(stream_key, dims, scale, most, shards=(), dtype=jnp.bfloat16):
    drawn = jax.random.normal(stream_key, dims, jnp.float32) * scale
    if len(shards) > 0:
        drawn = levels(stream_key, dims, shards, -0.22, 0.18) * drawn
    return jnp.clip(drawn, min=-most, max=most).astype(dtype)


def setup_inputs(seed: int = 0) -> dict:
    splits = jax.random.split(jax.random.key(seed), 11)
    return {
        "video_tokens": gaussian(splits[0], (VIDEO, D), 1.0, 6.0, ((0, 256),)),
        "text_tokens": gaussian(splits[1], (TEXT, D), 1.0, 6.0, ((0, 8),)),
        "video_modulation": gaussian(splits[2], (3, D), 0.8, 4.0),
        "text_modulation": gaussian(splits[3], (3, D), 0.8, 4.0),
        "video_projection": gaussian(splits[4], (D, 3, HEADS * HD), D ** -0.5, 0.109375, ((2, 8),)),
        "text_projection": gaussian(splits[5], (D, 3, HEADS * HD), D ** -0.5, 0.109375, ((2, 8),)),
        "video_output": gaussian(splits[6], (HEADS * HD, D), (HEADS * HD) ** -0.5, 0.125, ((0, 8),)),
        "text_output": gaussian(splits[7], (HEADS * HD, D), (HEADS * HD) ** -0.5, 0.125, ((0, 8),)),
        "video_gains": draw_video_gains(jax.random.fold_in(splits[10], 71), 0),
        "text_gains": draw_text_gains(jax.random.fold_in(splits[10], 71), 0),
    }


EPS_NORM = 1e-06

def modulate(rows, factors):
    floats = rows.astype(jnp.float32)
    centre = floats - lax.optimization_barrier(jnp.mean(floats, axis=-1, keepdims=True))
    spread = lax.optimization_barrier(jnp.mean(centre * centre, axis=-1, keepdims=True))
    normed = centre / jnp.sqrt(spread + EPS_NORM)
    wide = factors.astype(jnp.float32)
    return (normed * (1.0 + wide[1]) + wide[0]).astype(jnp.bfloat16)

def head_norm(vectors, channel_gain):
    inverse = lax.rsqrt(lax.optimization_barrier(jnp.mean(vectors * vectors, axis=-1, keepdims=True)) + EPS_NORM)
    return (vectors * inverse * channel_gain).astype(jnp.bfloat16)

def project(modded, weights, gains):
    mixture = jnp.einsum('td,dch->tch', modded.astype(jnp.float32), weights.astype(jnp.float32))
    row_count = mixture.shape[0]
    per_head = mixture.reshape(row_count, 3, mixture.shape[2] // HD, HD)
    query_rows = head_norm(per_head[:, 0], gains[0])
    key_rows = head_norm(per_head[:, 1], gains[1])
    value_rows = per_head[:, 2].astype(jnp.bfloat16)
    return (query_rows, key_rows, value_rows)

def attend(query_rows, key_rows, value_rows):
    total_rows = query_rows.shape[0]
    step_rows = math.gcd(total_rows, 512)
    query_blocks = query_rows.reshape(total_rows // step_rows, step_rows, query_rows.shape[1], HD)
    keys_wide = key_rows.astype(jnp.float32)
    values_wide = value_rows.astype(jnp.float32)

    def one_block(query_block):
        scores = jnp.einsum('qhd,khd->hqk', query_block.astype(jnp.float32), keys_wide) * HD ** (-0.5)
        highest = lax.optimization_barrier(jnp.max(scores, axis=-1, keepdims=True))
        weights = jnp.exp(scores - highest)
        totals = lax.optimization_barrier(jnp.sum(weights, axis=-1))
        rounded = weights.astype(jnp.bfloat16).astype(jnp.float32)
        mixture = jnp.einsum('hqk,khd->qhd', rounded, values_wide)
        return mixture / jnp.transpose(totals)[:, :, None]
    mixed_out = lax.map(one_block, query_blocks)
    return mixed_out.reshape(total_rows, query_rows.shape[1] * HD).astype(jnp.bfloat16)

def finish(heads_rows, weights, factors):
    group_cols = weights.shape[0] // N_ULY
    summed = jnp.zeros((heads_rows.shape[0], weights.shape[1]), jnp.float32)
    for group in range(N_ULY):
        partial_rows = jnp.dot(heads_rows[:, group * group_cols:(group + 1) * group_cols], weights[group * group_cols:(group + 1) * group_cols], preferred_element_type=jnp.float32)
        rounded = lax.optimization_barrier(partial_rows.astype(jnp.bfloat16))
        summed = summed + rounded.astype(jnp.float32)
    return (summed * factors[2].astype(jnp.float32)).astype(jnp.bfloat16)

def reference(video_tokens, text_tokens, video_modulation, text_modulation, video_projection, text_projection, video_output, text_output, video_gains, text_gains):
    video_query, video_key, video_value = project(modulate(video_tokens, video_modulation), video_projection, video_gains)
    text_query, text_key, text_value = project(modulate(text_tokens, text_modulation), text_projection, text_gains)
    joined_query = jnp.concatenate([video_query, text_query], axis=0)
    joined_key = jnp.concatenate([video_key, text_key], axis=0)
    joined_value = jnp.concatenate([video_value, text_value], axis=0)
    heads_out = attend(joined_query, joined_key, joined_value)
    video_count = video_tokens.shape[0]
    video_attention = finish(heads_out[:video_count], video_output, video_modulation)
    text_attention = finish(heads_out[video_count:], text_output, text_modulation)
    return (video_attention, text_attention)
```

```python
import math

import jax
import jax.numpy as jnp
from jax import lax
from jax.experimental import pallas as pl
from jax.experimental.pallas import tpu as pltpu
from jax.sharding import Mesh
from jax.sharding import PartitionSpec as P

D = 3072
HD = 128
EPS = 1e-06
MESH = pl.DeviceIdType.MESH
AX = ("x", "zl", "c", "y", "zh")
ULY = ("y", "zh")
CHUNK = 48
ROWS = 8 * CHUNK
TXT = 16
KEYS = 2 * ROWS
QT = 256
LOG2 = math.log2(math.e) / math.sqrt(HD)
F32 = jnp.float32
BF16 = jnp.bfloat16


class Place:
    def __init__(self):
        self.x, self.zl, self.c, self.y, self.zh = (lax.axis_index(a) for a in AX)

    def at(self, **moved):
        found = {"x": self.x, "zl": self.zl, "c": self.c, "y": self.y, "zh": self.zh}
        found.update(moved)
        return found

    def group(self, dy, dz):
        y = lax.rem(self.y + dy, 4)
        if dz:
            return self.at(y=y, zh=1 - self.zh, zl=3 - self.zl)
        return self.at(y=y)

    def text_home(self):
        level = jnp.where(self.zh == 0, self.zl, 3 - self.zl)
        high = level // 2
        home = {"y": self.x, "zh": high, "zl": jnp.where(high == 0, level, 3 - level)}
        here = jnp.logical_and(self.y == self.x, self.zh == high)
        return home, here, lax.rem(level, 2)


GROUP = [(dy, dz) for dz in (0, 1) for dy in range(4) if (dy, dz) != (0, 0)]


def greet(devices, more=0):
    barrier = pltpu.get_barrier_semaphore()
    for device in devices:
        pl.semaphore_signal(barrier, inc=1, device_id=device, device_id_type=MESH)
    return lambda: pl.semaphore_wait(barrier, len(devices) + more)


def remote(src, dst, ssem, rsem, device):
    return pltpu.make_async_remote_copy(
        src_ref=src, dst_ref=dst, send_sem=ssem, recv_sem=rsem,
        device_id=device, device_id_type=MESH,
    )


def modulate(rows, factors):
    floats = rows.astype(F32)
    centre = floats - jnp.mean(floats, axis=-1, keepdims=True)
    spread = jnp.mean(centre * centre, axis=-1, keepdims=True)
    normed = centre / jnp.sqrt(spread + EPS)
    return (normed * (1.0 + factors[1:2].astype(F32)) + factors[0:1].astype(F32)).astype(BF16)


def head_norm(vectors, gain):
    inverse = lax.rsqrt(jnp.mean(vectors * vectors, axis=-1, keepdims=True) + EPS)
    return (vectors * inverse * gain).astype(BF16)


def project_kernel(
    xv, xt, mv, mt, gv, gt, wv_hbm, wt_hbm, qkv, tqkv,
    rows, trow, wv, wt, wsem, ssem, rsem, tssem, trsem,
):
    me = Place()
    load_v = pltpu.make_async_copy(wv_hbm, wv, wsem.at[0])
    load_t = pltpu.make_async_copy(
        wt_hbm.at[:, :, pl.ds(pl.multiple_of(me.c * HD, HD), HD)], wt, wsem.at[1]
    )
    load_v.start()
    load_t.start()
    arrived = greet([me.group(dy, dz) for dy, dz in GROUP])
    rows[0] = modulate(xv[...], mv[...])
    _, home, half = me.text_home()

    @pl.when(home)
    def _():
        trow[...] = modulate(xt[pl.ds(pl.multiple_of(half * TXT, TXT), TXT), :], mt[...])

    arrived()

    def copy(src, dst, device):
        return remote(rows.at[src], rows.at[dst], ssem.at[dst], rsem.at[dst], device)

    up, down = me.group(1, 0), me.group(3, 0)
    far_src = 3 - 2 * me.c
    far_device = me.at(y=lax.rem(me.y + 1 + 2 * me.c, 4))

    mirror = copy(0, 4, me.group(0, 1))
    mirror.start()

    def spread(base):
        low, high = copy(base, base + 1, down), copy(base, base + 3, up)

        @pl.when(me.c == 0)
        def _():
            high.start()
            low.start()

        @pl.when(me.c == 1)
        def _():
            low.start()
            high.start()

        return low, high

    def onward(base, low, high):
        far = copy(base + far_src, base + 2, far_device)

        @pl.when(me.c == 0)
        def _():
            high.wait_recv()
            far.start()
            low.wait_recv()

        @pl.when(me.c == 1)
        def _():
            low.wait_recv()
            far.start()
            high.wait_recv()

        return far

    text_copies = [
        remote(trow, trow, tssem.at[i], trsem, me.group(dy, dz)) for i, (dy, dz) in enumerate(GROUP)
    ]
    first = spread(0)

    @pl.when(home)
    def _():
        for text_copy in text_copies:
            text_copy.start()

    def block(p):
        lhs = rows[4 * p : 4 * p + 4].reshape(4 * CHUNK, D)
        for j in range(3):
            total = jnp.dot(lhs, wv[j], preferred_element_type=F32)
            for h in range(2):
                part = total[:, h * HD : (h + 1) * HD]
                part = head_norm(part, gv[j : j + 1]) if j < 2 else part.astype(BF16)
                qkv[h, j, p * 4 * CHUNK : (p + 1) * 4 * CHUNK, :] = part

    far0 = onward(0, *first)
    mirror.wait_recv()
    second = spread(4)
    load_v.wait()
    far0.wait_recv()
    block(0)
    far1 = onward(4, *second)

    @pl.when(jnp.logical_not(home))
    def _():
        text_copies[0].wait_recv()

    load_t.wait()
    for j in range(3):
        part = jnp.dot(trow[...], wt[j], preferred_element_type=F32)
        tqkv[j] = head_norm(part, gt[j : j + 1]) if j < 2 else part.astype(BF16)
    far1.wait_recv()
    block(1)
    for sent in (mirror, *first, far0, *second, far1):
        sent.wait_send()

    @pl.when(home)
    def _():
        for text_copy in text_copies:
            text_copy.wait_send()


def vmem(n):
    return [pl.BlockSpec(memory_space=pltpu.VMEM)] * n


def hbm(n):
    return [pl.BlockSpec(memory_space=pl.ANY)] * n


DMA = pltpu.SemaphoreType.DMA


def project(xv, xt, mv, mt, gv, gt, wv, wt):
    return pl.pallas_call(
        project_kernel,
        out_shape=(
            jax.ShapeDtypeStruct((2, 3, ROWS, HD), BF16),
            jax.ShapeDtypeStruct((3, TXT, HD), BF16),
        ),
        in_specs=vmem(6) + hbm(2),
        out_specs=tuple(vmem(2)),
        scratch_shapes=[
            pltpu.VMEM((8, CHUNK, D), BF16),
            pltpu.VMEM((TXT, D), BF16),
            pltpu.VMEM((3, D, 2 * HD), BF16),
            pltpu.VMEM((3, D, HD), BF16),
            DMA((2,)), DMA((8,)), DMA((8,)), DMA((7,)), DMA,
        ],
        compiler_params=pltpu.CompilerParams(collective_id=0, has_side_effects=True),
        name="project",
    )(xv, xt, mv, mt, gv, gt, wv, wt)


def attend_kernel(
    qkv, tqkv, heads, theads,
    qb, kvb, tq, mb, lb, ab, ob, sb, tob, orecv, srecv, trecv,
    kvs, kvr, qs, qr, tks, tkr, tqs, tqr, os_, or_, ss, sr, ts, tr,
):
    me = Place()
    c = me.c
    other = 1 - c
    peers = [me.at(c=other)]
    for d in range(1, 4):
        for r in (c, other):
            peers.append(me.at(x=lax.rem(me.x + d, 4), c=r))
            peers.append(me.at(zl=lax.rem(me.zl + d, 4), c=r))
    arrived = greet(peers)

    def at_rows(core):
        return pl.ds(pl.multiple_of(core * ROWS, ROWS), ROWS)

    sends = []

    def send(copy):
        copy.start()
        sends.append(copy)

    local = [
        pltpu.make_async_copy(qkv.at[c, pl.ds(1, 2)], kvb.at[0, :, at_rows(c), :], kvr.at[0, 0]),
        pltpu.make_async_copy(qkv.at[c, 0], qb.at[0, at_rows(c), :], qr.at[0, 0]),
        pltpu.make_async_copy(tqkv.at[pl.ds(1, 2)], kvb.at[2, :, pl.ds(KEYS, TXT), :], tkr.at[0]),
        pltpu.make_async_copy(tqkv.at[0], tq.at[pl.ds(0, TXT), :], tqr.at[0]),
    ]
    for copy in local:
        copy.start()
    mb[...] = jnp.full_like(mb, -jnp.inf)
    lb[...] = jnp.zeros_like(lb)
    ab[...] = jnp.zeros_like(ab)
    arrived()

    def send_kv(d, r, i):
        slot = (4 - d) % 4
        send(remote(
            qkv.at[r, pl.ds(1, 2)], kvb.at[slot, :, at_rows(c), :],
            kvs.at[slot, i], kvr.at[slot, i], me.at(x=lax.rem(me.x + d, 4), c=r),
        ))

    def send_q(d, r, i):
        slot = (4 - d) % 4
        send(remote(
            qkv.at[r, 0], qb.at[slot, at_rows(c), :],
            qs.at[slot, i], qr.at[slot, i], me.at(zl=lax.rem(me.zl + d, 4), c=r),
        ))

    send_kv(0, other, 1)
    send_q(0, other, 1)
    for d in (1, 3, 2):
        for i, r in enumerate((c, other)):
            send_q(d, r, i)
        slot = (4 - d) % 4
        send(remote(
            tqkv.at[0], tq.at[pl.ds(TXT * slot, TXT), :], tqs.at[slot], tqr.at[slot],
            me.at(zl=lax.rem(me.zl + d, 4)),
        ))
        for i, r in enumerate((c, other)):
            send_kv(d, r, i)
        send(remote(
            tqkv.at[pl.ds(1, 2)], kvb.at[2, :, pl.ds(KEYS + TXT * slot, TXT), :],
            tks.at[slot], tkr.at[slot], me.at(x=lax.rem(me.x + d, 4)),
        ))

    def await_kv(slot):
        for i in range(2):
            rows = kvb.at[slot, :, pl.ds(i * ROWS, ROWS), :]
            pltpu.make_async_copy(rows, rows, kvr.at[slot, i]).wait()

    def await_q(slot):
        for i in range(2):
            rows = qb.at[slot, pl.ds(i * ROWS, ROWS), :]
            pltpu.make_async_copy(rows, rows, qr.at[slot, i]).wait()

    def gray(i):
        return i + jnp.where(i == 2, 1, 0) - jnp.where(i == 3, 1, 0)

    def step(queries, slot, count, at):
        keys = kvb[slot, 0, :count, :]
        values = kvb[slot, 1, :count, :]
        scores = lax.dot_general(
            queries, keys, (((1,), (1,)), ((), ())), preferred_element_type=F32
        )
        before = mb[at, :]
        now = jnp.maximum(before[:, :1], jnp.max(scores, axis=-1, keepdims=True))
        weights = jnp.exp2((scores - now) * LOG2)
        shrink = jnp.exp2((before - now) * LOG2)
        totals = lb[at, :] * shrink + jnp.sum(weights, axis=-1, keepdims=True)
        sums = ab[at, :] * shrink + jnp.dot(
            weights.astype(BF16), values, preferred_element_type=F32
        )
        return jnp.broadcast_to(now, sums.shape), totals, sums

    def keep(at, state):
        mb[at, :], lb[at, :], ab[at, :] = state

    tail = pl.ds(4 * KEYS, 4 * TXT)
    tiles = KEYS // QT

    def phase(i, _):
        slot = gray(i)
        await_kv(slot)

        def tile(n, _):
            q_slot = gray(n // tiles)
            part = lax.rem(n, tiles)

            @pl.when(jnp.logical_and(i == 0, part == 0))
            def _():
                await_q(q_slot)

            at = pl.ds(pl.multiple_of(q_slot * KEYS + part * QT, QT), QT)
            inner = pl.ds(pl.multiple_of(part * QT, QT), QT)
            keep(at, step(qb[q_slot, inner, :], slot, KEYS, at))
            return 0

        lax.fori_loop(0, 4 * tiles, tile, 0)

        @pl.when(i == 0)
        def _():
            for j in range(4):
                rows = tq.at[pl.ds(j * TXT, TXT), :]
                pltpu.make_async_copy(rows, rows, tqr.at[j]).wait()

        keep(tail, step(tq[...], slot, KEYS, tail))
        return 0

    lax.fori_loop(0, 3, phase, 0)
    await_kv(2)
    for j in range(4):
        rows = kvb.at[2, :, pl.ds(KEYS + j * TXT, TXT), :]
        pltpu.make_async_copy(rows, rows, tkr.at[j]).wait()
    count = KEYS + 4 * TXT

    highest, totals, sums = step(tq[...], 2, count, tail)
    tob[:, :HD] = sums / totals
    tob[:, HD:] = highest * LOG2 + jnp.log2(totals)
    for j in range(4):
        slot = (4 - j) % 4
        for i, r in enumerate((c, other)):
            src, dst = tob.at[pl.ds(TXT * j, TXT), :], trecv.at[slot, c]
            if j == 0 and i == 0:
                mine_t = pltpu.make_async_copy(src, dst, tr.at[0, 0])
                mine_t.start()
            else:
                send(remote(src, dst, ts.at[slot, i], tr.at[slot, i],
                            me.at(zl=lax.rem(me.zl + j, 4), c=r)))

    def out_copies(j, slot, i, r):
        device = me.at(zl=lax.rem(me.zl + j, 4), c=r)
        at = pl.ds(pl.multiple_of(r * ROWS, ROWS), ROWS)
        return (
            remote(ob.at[j, at, :], orecv.at[slot, c], os_.at[slot, i], or_.at[slot, i], device),
            remote(sb.at[j, :, at], srecv.at[slot, c], ss.at[slot, i], sr.at[slot, i], device),
        )

    mine = (
        pltpu.make_async_copy(ob.at[0, at_rows(c), :], orecv.at[0, c], or_.at[0, 0]),
        pltpu.make_async_copy(sb.at[0, :, at_rows(c)], srecv.at[0, c], sr.at[0, 0]),
    )

    def last(n, _):
        q_slot = gray(3 - n // tiles)
        part = lax.rem(n, tiles)
        at = pl.ds(pl.multiple_of(q_slot * KEYS + part * QT, QT), QT)
        inner = pl.ds(pl.multiple_of(part * QT, QT), QT)
        highest, totals, sums = step(qb[q_slot, inner, :], 2, count, at)
        ob[q_slot, inner, :] = (sums / totals).astype(BF16)
        level = highest * LOG2 + jnp.log2(totals)
        sb[q_slot, :, inner] = jnp.transpose(level)[:8, :]

        @pl.when(jnp.logical_and(part == tiles - 1, q_slot > 0))
        def _():
            for i, r in enumerate((c, other)):
                for copy in out_copies(q_slot, 4 - q_slot, i, r):
                    copy.start()

        @pl.when(jnp.logical_and(part == tiles - 1, q_slot == 0))
        def _():
            for copy in out_copies(0, 0, 1, other):
                copy.start()
            for copy in mine:
                copy.start()

        return 0

    lax.fori_loop(0, 4 * tiles, last, 0)
    for copy in sends:
        copy.wait_send()
    for slot in range(4):
        for i, r in enumerate((c, other)):
            dst = trecv.at[slot, r]
            pltpu.make_async_copy(dst, dst, tr.at[slot, i]).wait()
    for h in range(2):
        found = [trecv[slot, h] for slot in range(4)]
        top = found[0][:, HD:]
        for part in found[1:]:
            top = jnp.maximum(top, part[:, HD:])
        weight = [jnp.exp2(part[:, HD:] - top) for part in found]
        mixed = sum(w * part[:, :HD] for w, part in zip(weight, found)) / sum(weight)
        theads[:, h * HD : (h + 1) * HD] = mixed.astype(BF16)
    for slot in range(4):
        for i, r in enumerate((c, other)):
            for dst, sems in ((orecv.at[slot, r], or_), (srecv.at[slot, r], sr)):
                pltpu.make_async_copy(dst, dst, sems.at[slot, i]).wait()
    for h in range(2):
        found = [srecv[slot, h] for slot in range(4)]
        top = jnp.maximum(jnp.maximum(found[0], found[1]), jnp.maximum(found[2], found[3]))
        weight = [jnp.exp2(part - top) for part in found]
        share = 1.0 / sum(weight)
        mixed = jnp.zeros((ROWS, HD), F32)
        for slot in range(4):
            row = (weight[slot] * share)[:1]
            column = jnp.transpose(jnp.broadcast_to(row, (HD, ROWS)))
            mixed = mixed + column * orecv[slot, h].astype(F32)
        heads[:, h * HD : (h + 1) * HD] = mixed.astype(BF16)
    for slot in range(4):
        for i, r in enumerate((c, other)):
            if (slot, i) != (0, 0):
                for copy in out_copies((4 - slot) % 4, slot, i, r):
                    copy.wait_send()


def attend(qkv, tqkv):
    return pl.pallas_call(
        attend_kernel,
        out_shape=(
            jax.ShapeDtypeStruct((ROWS, 2 * HD), BF16),
            jax.ShapeDtypeStruct((TXT, 2 * HD), BF16),
        ),
        in_specs=vmem(2),
        out_specs=tuple(vmem(2)),
        scratch_shapes=[
            pltpu.VMEM((4, KEYS, HD), BF16),
            pltpu.VMEM((4, 2, KEYS + 4 * TXT, HD), BF16),
            pltpu.VMEM((4 * TXT, HD), BF16),
            pltpu.VMEM((4 * KEYS + 4 * TXT, HD), F32),
            pltpu.VMEM((4 * KEYS + 4 * TXT, HD), F32),
            pltpu.VMEM((4 * KEYS + 4 * TXT, HD), F32),
            pltpu.VMEM((4, KEYS, HD), BF16),
            pltpu.VMEM((4, 8, KEYS), F32),
            pltpu.VMEM((4 * TXT, 2 * HD), F32),
            pltpu.VMEM((4, 2, ROWS, HD), BF16),
            pltpu.VMEM((4, 2, 8, ROWS), F32),
            pltpu.VMEM((4, 2, TXT, 2 * HD), F32),
        ]
        + [DMA((4, 2))] * 4 + [DMA((4,))] * 4 + [DMA((4, 2))] * 6,
        compiler_params=pltpu.CompilerParams(collective_id=1, has_side_effects=True),
        name="attend",
    )(qkv, tqkv)


def finish_kernel(
    heads, theads, mv, mt, wv_hbm, wt_hbm, video_out, text_out,
    pb, fb, nb, zb, zs, tp, trb, tfin, tpiece, wv, wt,
    wsem, fs, fr, ns, nr, zsem, zr, tss, trs, bs, br,
):
    me = Place()
    c = me.c
    half_cols = D // 2
    load_v = pltpu.make_async_copy(wv_hbm, wv, wsem.at[0])
    cols = pl.ds(pl.multiple_of(c * half_cols, half_cols), half_cols)
    load_t = pltpu.make_async_copy(wt_hbm.at[:, cols], wt, wsem.at[1])
    load_v.start()
    load_t.start()
    lin = (me.x * 4 + me.zl) * 2 + c

    def plane(k):
        n = lax.rem(lin + k, 32)
        return me.at(x=n // 8, zl=lax.rem(n // 2, 4), c=lax.rem(n, 2))

    arrived = greet([me.group(dy, dz) for dy, dz in GROUP], 31)
    barrier = pltpu.get_barrier_semaphore()

    def hello(k, _):
        pl.semaphore_signal(barrier, inc=1, device_id=plane(k), device_id_type=MESH)
        return 0

    lax.fori_loop(1, 32, hello, 0)
    home_at, home, _ = me.text_home()
    mine = me.y * 2 + me.zh

    load_t.wait()
    part = jnp.dot(theads[...], wt[...], preferred_element_type=F32).astype(BF16)
    tp[...] = part
    load_v.wait()
    for p in (1, 0):
        lhs = heads[p * 4 * CHUNK : (p + 1) * 4 * CHUNK, :]
        for q in range(4):
            span = slice(q * (D // 4), (q + 1) * (D // 4))
            found = jnp.dot(lhs, wv[:, span], preferred_element_type=F32).astype(BF16)
            pb[4 * p : 4 * p + 4, :, span] = found.reshape(4, CHUNK, D // 4)
    arrived()

    gather_text = remote(tp, trb.at[mine], tss.at[0], trs.at[mine], me.at(**home_at))

    @pl.when(jnp.logical_not(home))
    def _():
        gather_text.start()

    up, down = me.group(1, 0), me.group(3, 0)
    far_device = me.at(y=lax.rem(me.y + 3 + 2 * c, 4))
    near_device = far_device
    near_slot = 3 - 2 * c
    plain_device = me.at(y=lax.rem(me.y + 1 + 2 * c, 4))
    plain_slot = 1 + 2 * c

    def far_copy(p):
        return remote(pb.at[4 * p + 2], fb.at[p], fs.at[p], fr.at[p], far_device)

    def plain_copy(p):
        return remote(pb.at[4 * p + plain_slot], nb.at[p, 0], ns.at[p, 0], nr.at[p, 0], plain_device)

    def sum_copy(p):
        return remote(pb.at[4 * p + near_slot], nb.at[p, 1], ns.at[p, 1], nr.at[p, 1], near_device)

    for p in (1, 0):
        far_copy(p).start()
        plain_copy(p).start()

    def relay(p):
        far_copy(p).wait_recv()
        total = pb[4 * p + near_slot].astype(F32) + fb[p].astype(F32)
        pb[4 * p + near_slot] = total.astype(BF16)
        sum_copy(p).start()

    def collect(p):
        plain_copy(p).wait_recv()
        sum_copy(p).wait_recv()
        return pb[4 * p].astype(F32) + nb[p, 0].astype(F32) + nb[p, 1].astype(F32)

    mirror = remote(zs, zb, zsem, zr, me.group(0, 1))
    relay(1)
    zs[...] = collect(1).astype(BF16)
    mirror.start()

    level = jnp.where(me.zh == 0, me.zl, 3 - me.zl)

    def piece_copy(k):
        return remote(
            tfin, tpiece.at[lax.rem(level, 2), c],
            bs.at[k - 1], br.at[lax.rem(level, 2), c], plane(k),
        )

    @pl.when(home)
    def _():
        total = tp[...].astype(F32)
        for s in range(8):
            @pl.when(s != mine)
            def _():
                pltpu.make_async_copy(trb.at[s], trb.at[s], trs.at[s]).wait()

            @pl.when(s == mine)
            def _():
                trb[s] = tp[...]

        total = trb[0].astype(F32)
        for s in range(1, 8):
            total = total + trb[s].astype(F32)
        gate = mt[2:3, cols].astype(F32)
        tfin[...] = (total * gate).astype(BF16)

        def out(k, _):
            piece_copy(k).start()
            return 0

        lax.fori_loop(1, 32, out, 0)
        tpiece[lax.rem(level, 2), c] = tfin[...]

    relay(0)
    summed = collect(0)
    mirror.wait_recv()
    summed = summed + zb[...].astype(F32)
    video_out[...] = (summed * mv[2:3].astype(F32)).astype(BF16)

    for b in range(2):
        for r in range(2):
            @pl.when(jnp.logical_not(jnp.logical_and(home, jnp.logical_and(lax.rem(level, 2) == b, c == r))))
            def _():
                pltpu.make_async_copy(tpiece.at[b, r], tpiece.at[b, r], br.at[b, r]).wait()
            text_out[b * TXT : (b + 1) * TXT, r * half_cols : (r + 1) * half_cols] = tpiece[b, r]
    for p in (0, 1):
        far_copy(p).wait_send()
        plain_copy(p).wait_send()
        sum_copy(p).wait_send()
    mirror.wait_send()

    @pl.when(jnp.logical_not(home))
    def _():
        gather_text.wait_send()

    @pl.when(home)
    def _():
        def done(k, _):
            piece_copy(k).wait_send()
            return 0

        lax.fori_loop(1, 32, done, 0)


def finish(heads, theads, mv, mt, wv, wt):
    half_cols = D // 2
    return pl.pallas_call(
        finish_kernel,
        out_shape=(
            jax.ShapeDtypeStruct((CHUNK, D), BF16),
            jax.ShapeDtypeStruct((2 * TXT, D), BF16),
        ),
        in_specs=vmem(4) + hbm(2),
        out_specs=tuple(vmem(2)),
        scratch_shapes=[
            pltpu.VMEM((8, CHUNK, D), BF16),
            pltpu.VMEM((2, CHUNK, D), BF16),
            pltpu.VMEM((2, 2, CHUNK, D), BF16),
            pltpu.VMEM((CHUNK, D), BF16),
            pltpu.VMEM((CHUNK, D), BF16),
            pltpu.VMEM((TXT, half_cols), BF16),
            pltpu.VMEM((8, TXT, half_cols), BF16),
            pltpu.VMEM((TXT, half_cols), BF16),
            pltpu.VMEM((2, 2, TXT, half_cols), BF16),
            pltpu.VMEM((2 * HD, D), BF16),
            pltpu.VMEM((2 * HD, half_cols), BF16),
            DMA((2,)), DMA((2,)), DMA((2,)), DMA((2, 2)), DMA((2, 2)), DMA, DMA,
            DMA((1,)), DMA((8,)), DMA((31,)), DMA((2, 2)),
        ],
        compiler_params=pltpu.CompilerParams(collective_id=2, has_side_effects=True),
        name="finish",
    )(heads, theads, mv, mt, wv, wt)


def local(
    video_tokens, text_tokens, video_modulation, text_modulation, video_projection,
    text_projection, video_output, text_output, video_gains, text_gains,
):
    qkv, tqkv = project(
        video_tokens, text_tokens, video_modulation, text_modulation, video_gains, text_gains,
        jnp.transpose(video_projection, (1, 0, 2)), jnp.transpose(text_projection, (1, 0, 2)),
    )
    heads, theads = attend(qkv, tqkv)
    return finish(heads, theads, video_modulation, text_modulation, video_output, text_output)


def solution(mesh):
    torus = Mesh(mesh.devices.reshape(4, 4, 2, 4, 2), AX)
    placed = (
        P(AX, None),
        P(ULY, None),
        P(),
        P(),
        P(None, None, ULY),
        P(None, None, ULY),
        P(ULY, None),
        P(ULY, None),
        P(),
        P(),
    )
    return jax.shard_map(
        local,
        mesh=torus,
        in_specs=placed,
        out_specs=(P(AX, None), P(ULY, None)),
        check_vma=False,
    )
```

```python
import math

import jax
import jax.numpy as jnp
from jax import lax
from jax.experimental import pallas as pl
from jax.experimental.pallas import tpu as pltpu
from jax.sharding import Mesh
from jax.sharding import PartitionSpec as P

D = 3072
HD = 128
EPS = 1e-06
MESH = pl.DeviceIdType.MESH
AX = ("x", "zl", "c", "y", "zh")
ULY = ("y", "zh")
CHUNK = 48
ROWS = 8 * CHUNK
TXT = 16
KEYS = 2 * ROWS
QT = 384
LOG2 = math.log2(math.e) / math.sqrt(HD)
F32 = jnp.float32
BF16 = jnp.bfloat16


class Place:
    def __init__(self):
        self.x, self.zl, self.c, self.y, self.zh = (lax.axis_index(a) for a in AX)

    def at(self, **moved):
        found = {"x": self.x, "zl": self.zl, "c": self.c, "y": self.y, "zh": self.zh}
        found.update(moved)
        return found

    def group(self, dy, dz):
        y = lax.rem(self.y + dy, 4)
        if dz:
            return self.at(y=y, zh=1 - self.zh, zl=3 - self.zl)
        return self.at(y=y)

    def piece(self):
        return lax.rem(self.y + self.x, 4), jnp.where(self.zl < 2, self.zh, 1 - self.zh), lax.rem(self.zl, 2)


GROUP = [(dy, dz) for dz in (0, 1) for dy in range(4) if (dy, dz) != (0, 0)]


def greet(devices, more=0):
    barrier = pltpu.get_barrier_semaphore()
    for device in devices:
        pl.semaphore_signal(barrier, inc=1, device_id=device, device_id_type=MESH)
    return lambda: pl.semaphore_wait(barrier, len(devices) + more)


def remote(src, dst, ssem, rsem, device):
    return pltpu.make_async_remote_copy(
        src_ref=src, dst_ref=dst, send_sem=ssem, recv_sem=rsem,
        device_id=device, device_id_type=MESH,
    )


def modulate(rows, factors):
    floats = rows.astype(F32)
    centre = floats - jnp.mean(floats, axis=-1, keepdims=True)
    spread = jnp.mean(centre * centre, axis=-1, keepdims=True)
    normed = centre / jnp.sqrt(spread + EPS)
    return (normed * (1.0 + factors[1:2].astype(F32)) + factors[0:1].astype(F32)).astype(BF16)


def head_norm(vectors, gain):
    inverse = lax.rsqrt(jnp.mean(vectors * vectors, axis=-1, keepdims=True) + EPS)
    return (vectors * inverse * gain).astype(BF16)


def project_kernel(
    xv, xt, mv, mt, gv, gt, wv_hbm, wt_hbm, qkv, tqkv,
    rows, ttmp, trow, wv, wt, wsem, ssem, rsem, tssem, trsem,
):
    me = Place()
    load_v = pltpu.make_async_copy(wv_hbm, wv, wsem.at[0])
    load_t = pltpu.make_async_copy(
        wt_hbm.at[:, :, pl.ds(pl.multiple_of(me.c * HD, HD), HD)], wt, wsem.at[1]
    )
    load_v.start()
    load_t.start()
    arrived = greet([me.group(dy, dz) for dy, dz in GROUP])
    rows[0] = modulate(xv[...], mv[...])
    low_chip = me.zl < 2
    stays = jnp.logical_and(low_chip, me.x == 0)

    @pl.when(low_chip)
    def _():
        for b in range(2):
            ttmp[b] = modulate(xt[b * TXT : (b + 1) * TXT, :], mt[...])

    @pl.when(stays)
    def _():
        trow[...] = ttmp[me.zl]

    arrived()

    def copy(src, dst, device):
        return remote(rows.at[src], rows.at[dst], ssem.at[dst], rsem.at[dst], device)

    up, down = me.group(1, 0), me.group(3, 0)
    far_src = 3 - 2 * me.c
    far_device = me.at(y=lax.rem(me.y + 1 + 2 * me.c, 4))

    mirror = copy(0, 4, me.group(0, 1))
    mirror.start()

    def spread(base):
        low, high = copy(base, base + 1, down), copy(base, base + 3, up)

        @pl.when(me.c == 0)
        def _():
            high.start()
            low.start()

        @pl.when(me.c == 1)
        def _():
            low.start()
            high.start()

        return low, high

    def onward(base, low, high):
        far = copy(base + far_src, base + 2, far_device)

        @pl.when(me.c == 0)
        def _():
            high.wait_recv()
            far.start()
            low.wait_recv()

        @pl.when(me.c == 1)
        def _():
            low.wait_recv()
            far.start()
            high.wait_recv()

        return far

    text_y = lax.rem(me.y + 4 - me.x, 4)
    text_near = remote(ttmp.at[lax.rem(me.zl, 2)], trow, tssem.at[0], trsem, me.at(y=text_y))
    text_over = remote(
        ttmp.at[1 - lax.rem(me.zl, 2)], trow, tssem.at[1], trsem,
        me.at(y=text_y, zh=1 - me.zh, zl=3 - me.zl),
    )
    first = spread(0)

    @pl.when(low_chip)
    def _():
        text_over.start()

    @pl.when(jnp.logical_and(low_chip, me.x > 0))
    def _():
        text_near.start()

    def block(p):
        lhs = rows[4 * p : 4 * p + 4].reshape(4 * CHUNK, D)
        for j in range(3):
            total = jnp.dot(lhs, wv[j], preferred_element_type=F32)
            for h in range(2):
                part = total[:, h * HD : (h + 1) * HD]
                part = head_norm(part, gv[j : j + 1]) if j < 2 else part.astype(BF16)
                qkv[h, j, p * 4 * CHUNK : (p + 1) * 4 * CHUNK, :] = part

    far0 = onward(0, *first)
    mirror.wait_recv()
    second = spread(4)
    load_v.wait()
    far0.wait_recv()
    block(0)
    far1 = onward(4, *second)

    @pl.when(jnp.logical_not(stays))
    def _():
        text_near.wait_recv()

    load_t.wait()
    for j in range(3):
        part = jnp.dot(trow[...], wt[j], preferred_element_type=F32)
        tqkv[j] = head_norm(part, gt[j : j + 1]) if j < 2 else part.astype(BF16)
    far1.wait_recv()
    block(1)
    for sent in (mirror, *first, far0, *second, far1):
        sent.wait_send()

    @pl.when(low_chip)
    def _():
        text_over.wait_send()

    @pl.when(jnp.logical_and(low_chip, me.x > 0))
    def _():
        text_near.wait_send()


def vmem(n):
    return [pl.BlockSpec(memory_space=pltpu.VMEM)] * n


def hbm(n):
    return [pl.BlockSpec(memory_space=pl.ANY)] * n


DMA = pltpu.SemaphoreType.DMA


def project(xv, xt, mv, mt, gv, gt, wv, wt):
    return pl.pallas_call(
        project_kernel,
        out_shape=(
            jax.ShapeDtypeStruct((2, 3, ROWS, HD), BF16),
            jax.ShapeDtypeStruct((3, TXT, HD), BF16),
        ),
        in_specs=vmem(6) + hbm(2),
        out_specs=tuple(vmem(2)),
        scratch_shapes=[
            pltpu.VMEM((8, CHUNK, D), BF16),
            pltpu.VMEM((2, TXT, D), BF16),
            pltpu.VMEM((TXT, D), BF16),
            pltpu.VMEM((3, D, 2 * HD), BF16),
            pltpu.VMEM((3, D, HD), BF16),
            DMA((2,)), DMA((8,)), DMA((8,)), DMA((2,)), DMA,
        ],
        compiler_params=pltpu.CompilerParams(collective_id=0, has_side_effects=True),
        name="project",
    )(xv, xt, mv, mt, gv, gt, wv, wt)


def attend_kernel(
    qkv, tqkv, heads, theads,
    qb, kva, kvb, tq, mb, lb, ab, ob, sb, tob, orecv, srecv, trecv,
    kvs, kvr, qs, qr, tks, tkr, tqs, tqr, os_, or_, ss, sr, ts, tr,
):
    me = Place()
    c = me.c
    other = 1 - c
    peers = [me.at(c=other)]
    for d in range(1, 4):
        for r in (c, other):
            peers.append(me.at(x=lax.rem(me.x + d, 4), c=r))
            peers.append(me.at(zl=lax.rem(me.zl + d, 4), c=r))
    arrived = greet(peers)

    def at_rows(core):
        return pl.ds(pl.multiple_of(core * ROWS, ROWS), ROWS)

    sends = []

    def send(copy):
        copy.start()
        sends.append(copy)

    def kv_rows(slot, core):
        buf = kva if slot in (0, 1) else kvb
        base = 0 if slot in (0, 3) else KEYS
        return buf.at[:, pl.ds(pl.multiple_of(base + core * ROWS, ROWS), ROWS), :]

    def kv_text(slot):
        return kvb.at[:, pl.ds(2 * KEYS + TXT * slot, TXT), :]

    local = [
        pltpu.make_async_copy(qkv.at[c, pl.ds(1, 2)], kv_rows(0, c), kvr.at[0, 0]),
        pltpu.make_async_copy(qkv.at[c, 0], qb.at[0, at_rows(c), :], qr.at[0, 0]),
        pltpu.make_async_copy(tqkv.at[pl.ds(1, 2)], kv_text(0), tkr.at[0]),
        pltpu.make_async_copy(tqkv.at[0], tq.at[pl.ds(0, TXT), :], tqr.at[0]),
    ]
    for copy in local:
        copy.start()
    arrived()

    def send_kv(d, r, i):
        slot = (4 - d) % 4
        send(remote(
            qkv.at[r, pl.ds(1, 2)], kv_rows(slot, c),
            kvs.at[slot, i], kvr.at[slot, i], me.at(x=lax.rem(me.x + d, 4), c=r),
        ))

    def send_q(d, r, i):
        slot = (4 - d) % 4
        send(remote(
            qkv.at[r, 0], qb.at[slot, at_rows(c), :],
            qs.at[slot, i], qr.at[slot, i], me.at(zl=lax.rem(me.zl + d, 4), c=r),
        ))

    send_kv(0, other, 1)
    send_q(0, other, 1)
    for d in (3, 1, 2):
        for i, r in enumerate((c, other)):
            send_q(d, r, i)
        slot = (4 - d) % 4
        send(remote(
            tqkv.at[0], tq.at[pl.ds(TXT * slot, TXT), :], tqs.at[slot], tqr.at[slot],
            me.at(zl=lax.rem(me.zl + d, 4)),
        ))
        for i, r in enumerate((c, other)):
            send_kv(d, r, i)
        send(remote(
            tqkv.at[pl.ds(1, 2)], kv_text(slot),
            tks.at[slot], tkr.at[slot], me.at(x=lax.rem(me.x + d, 4)),
        ))

    def await_kv(slot):
        for i in range(2):
            rows = kv_rows(slot, i)
            pltpu.make_async_copy(rows, rows, kvr.at[slot, i]).wait()

    def await_q(slot):
        for i in range(2):
            rows = qb.at[slot, pl.ds(i * ROWS, ROWS), :]
            pltpu.make_async_copy(rows, rows, qr.at[slot, i]).wait()

    def gray(i):
        return i + jnp.where(i == 2, 1, 0) - jnp.where(i == 3, 1, 0)

    def scored(queries, keys):
        return lax.dot_general(
            queries, keys, (((1,), (1,)), ((), ())), preferred_element_type=F32
        )

    def lanes(weights):
        width = weights.shape[1]
        if width % HD:
            extra = weights[:, width - width % HD :]
            pad = jnp.zeros((extra.shape[0], HD - width % HD), F32)
            total = jnp.concatenate([extra, pad], axis=1)
        else:
            total = jnp.zeros((weights.shape[0], HD), F32)
        for k in range(width // HD):
            total = total + weights[:, k * HD : (k + 1) * HD]
        return total

    def open_step(queries, at):
        scores = scored(queries, kva[0])
        now = jnp.max(scores, axis=-1, keepdims=True)
        weights = jnp.exp2((scores - now) * LOG2)
        mb[at, :] = jnp.broadcast_to(now, (queries.shape[0], HD))
        lb[at, :] = lanes(weights)
        ab[at, :] = jnp.dot(weights.astype(BF16), kva[1], preferred_element_type=F32)

    def last_step(queries, at):
        scores = scored(queries, kvb[0])
        before = mb[at, :]
        now = jnp.maximum(before[:, :1], jnp.max(scores, axis=-1, keepdims=True))
        weights = jnp.exp2((scores - now) * LOG2)
        shrink = jnp.exp2((before - now) * LOG2)
        totals = jnp.sum(lb[at, :] * shrink + lanes(weights), axis=-1, keepdims=True)
        sums = ab[at, :] * shrink + jnp.dot(
            weights.astype(BF16), kvb[1], preferred_element_type=F32
        )
        level = jnp.broadcast_to(now * LOG2 + jnp.log2(totals), sums.shape)
        return sums / totals, level

    tail = pl.ds(4 * KEYS, 4 * TXT)

    await_kv(0)
    await_kv(1)

    def open_slot(i, _):
        q_slot = gray(i)
        await_q(q_slot)
        for part in range(KEYS // QT):
            at = pl.ds(pl.multiple_of(q_slot * KEYS + part * QT, QT), QT)
            open_step(qb[q_slot, part * QT : (part + 1) * QT, :], at)
        return 0

    lax.fori_loop(0, 4, open_slot, 0)
    for j in range(4):
        rows = tq.at[pl.ds(j * TXT, TXT), :]
        pltpu.make_async_copy(rows, rows, tqr.at[j]).wait()
    open_step(tq[...], tail)
    await_kv(3)
    await_kv(2)
    for j in range(4):
        pltpu.make_async_copy(kv_text(j), kv_text(j), tkr.at[j]).wait()

    mixed, level = last_step(tq[...], tail)
    tob[:, :HD] = mixed
    tob[:, HD:] = level
    for j in range(4):
        slot = (4 - j) % 4
        for i, r in enumerate((c, other)):
            src, dst = tob.at[pl.ds(TXT * j, TXT), :], trecv.at[slot, c]
            if j == 0 and i == 0:
                mine_t = pltpu.make_async_copy(src, dst, tr.at[0, 0])
                mine_t.start()
            else:
                send(remote(src, dst, ts.at[slot, i], tr.at[slot, i],
                            me.at(zl=lax.rem(me.zl + j, 4), c=r)))

    def out_copies(j, slot, i, r):
        device = me.at(zl=lax.rem(me.zl + j, 4), c=r)
        at = pl.ds(pl.multiple_of(r * ROWS, ROWS), ROWS)
        return (
            remote(ob.at[j, at, :], orecv.at[slot, c], os_.at[slot, i], or_.at[slot, i], device),
            remote(sb.at[j, :, at], srecv.at[slot, c], ss.at[slot, i], sr.at[slot, i], device),
        )

    mine = (
        pltpu.make_async_copy(ob.at[0, at_rows(c), :], orecv.at[0, c], or_.at[0, 0]),
        pltpu.make_async_copy(sb.at[0, :, at_rows(c)], srecv.at[0, c], sr.at[0, 0]),
    )

    def last_slot(n, _):
        q_slot = gray(3 - n)
        for part in range(KEYS // QT):
            at = pl.ds(pl.multiple_of(q_slot * KEYS + part * QT, QT), QT)
            inner = slice(part * QT, (part + 1) * QT)
            mixed, level = last_step(qb[q_slot, inner, :], at)
            ob[q_slot, inner, :] = mixed.astype(BF16)
            sb[q_slot, :, inner] = jnp.transpose(level)[:8, :]

        @pl.when(q_slot > 0)
        def _():
            for i, r in enumerate((c, other)):
                for copy in out_copies(q_slot, 4 - q_slot, i, r):
                    copy.start()

        @pl.when(q_slot == 0)
        def _():
            for copy in out_copies(0, 0, 1, other):
                copy.start()
            for copy in mine:
                copy.start()

        return 0

    lax.fori_loop(0, 4, last_slot, 0)
    for copy in sends:
        copy.wait_send()
    for slot in range(4):
        for i, r in enumerate((c, other)):
            dst = trecv.at[slot, r]
            pltpu.make_async_copy(dst, dst, tr.at[slot, i]).wait()
    for h in range(2):
        found = [trecv[slot, h] for slot in range(4)]
        top = found[0][:, HD:]
        for part in found[1:]:
            top = jnp.maximum(top, part[:, HD:])
        weight = [jnp.exp2(part[:, HD:] - top) for part in found]
        mixed = sum(w * part[:, :HD] for w, part in zip(weight, found)) / sum(weight)
        theads[:, h * HD : (h + 1) * HD] = mixed.astype(BF16)
    for slot in range(4):
        for i, r in enumerate((c, other)):
            for dst, sems in ((orecv.at[slot, r], or_), (srecv.at[slot, r], sr)):
                pltpu.make_async_copy(dst, dst, sems.at[slot, i]).wait()
    for h in range(2):
        found = [srecv[slot, h] for slot in range(4)]
        top = jnp.maximum(jnp.maximum(found[0], found[1]), jnp.maximum(found[2], found[3]))
        weight = [jnp.exp2(part - top) for part in found]
        share = 1.0 / sum(weight)
        mixed = jnp.zeros((ROWS, HD), F32)
        for slot in range(4):
            row = (weight[slot] * share)[:1]
            column = jnp.transpose(jnp.broadcast_to(row, (HD, ROWS)))
            mixed = mixed + column * orecv[slot, h].astype(F32)
        heads[:, h * HD : (h + 1) * HD] = mixed.astype(BF16)
    for slot in range(4):
        for i, r in enumerate((c, other)):
            if (slot, i) != (0, 0):
                for copy in out_copies((4 - slot) % 4, slot, i, r):
                    copy.wait_send()


def attend(qkv, tqkv):
    return pl.pallas_call(
        attend_kernel,
        out_shape=(
            jax.ShapeDtypeStruct((ROWS, 2 * HD), BF16),
            jax.ShapeDtypeStruct((TXT, 2 * HD), BF16),
        ),
        in_specs=vmem(2),
        out_specs=tuple(vmem(2)),
        scratch_shapes=[
            pltpu.VMEM((4, KEYS, HD), BF16),
            pltpu.VMEM((2, 2 * KEYS, HD), BF16),
            pltpu.VMEM((2, 2 * KEYS + 4 * TXT, HD), BF16),
            pltpu.VMEM((4 * TXT, HD), BF16),
            pltpu.VMEM((4 * KEYS + 4 * TXT, HD), F32),
            pltpu.VMEM((4 * KEYS + 4 * TXT, HD), F32),
            pltpu.VMEM((4 * KEYS + 4 * TXT, HD), F32),
            pltpu.VMEM((4, KEYS, HD), BF16),
            pltpu.VMEM((4, 8, KEYS), F32),
            pltpu.VMEM((4 * TXT, 2 * HD), F32),
            pltpu.VMEM((4, 2, ROWS, HD), BF16),
            pltpu.VMEM((4, 2, 8, ROWS), F32),
            pltpu.VMEM((4, 2, TXT, 2 * HD), F32),
        ]
        + [DMA((4, 2))] * 4 + [DMA((4,))] * 4 + [DMA((4, 2))] * 6,
        compiler_params=pltpu.CompilerParams(collective_id=1, has_side_effects=True),
        name="attend",
    )(qkv, tqkv)


def finish_kernel(
    heads, theads, mv, mt, wv_hbm, wt_hbm, video_out, text_out,
    pb, fb, nb, zb, zs, tp, trb, tfin, tall, wv, wt,
    wsem, fs, fr, ns, nr, zsem, zr, tss, trs, bs, br, xs, xr,
):
    me = Place()
    c = me.c
    half_cols = D // 2
    load_v = pltpu.make_async_copy(wv_hbm, wv, wsem.at[0])
    cols = pl.ds(pl.multiple_of(c * half_cols, half_cols), half_cols)
    load_t = pltpu.make_async_copy(wt_hbm.at[:, cols], wt, wsem.at[1])
    load_v.start()
    load_t.start()
    piece_y, piece_zh, half = me.piece()
    mine = me.y * 2 + me.zh
    home = me.zl // 2 == c

    def gatherer(k):
        return me.at(x=k, zl=2 * c + half, y=piece_y, zh=piece_zh)

    def giver(s):
        y, zh = s // 2, s % 2
        side = jnp.where(me.zh == zh, 0, 1)
        return me.at(x=lax.rem(me.y + 4 - y, 4), zl=2 * side + half, y=y, zh=zh)

    own_piece = jnp.logical_and(me.x == 0, jnp.logical_and(me.zl < 2, c == 0))
    column = [me.at(zl=lax.rem(me.zl + d, 4), c=r) for d in range(4) for r in (c, 1 - c)]
    across = [me.at(x=lax.rem(me.x + d, 4)) for d in range(1, 4)]
    up, down = me.group(1, 0), me.group(3, 0)
    arrived = greet(
        [up, down, me.group(0, 1)] + column[1:] + across,
        4 - jnp.where(own_piece, 1, 0),
    )
    barrier = pltpu.get_barrier_semaphore()

    @pl.when(home)
    def _():
        for s in range(8):
            @pl.when(jnp.logical_not(jnp.logical_and(own_piece, s == mine)))
            def _():
                pl.semaphore_signal(barrier, inc=1, device_id=giver(s), device_id_type=MESH)

    load_t.wait()
    part = jnp.dot(theads[...], wt[...], preferred_element_type=F32).astype(BF16)
    for k in range(4):
        tp[k] = part[:, k * (D // 8) : (k + 1) * (D // 8)]
    load_v.wait()
    for p in (1, 0):
        lhs = heads[p * 4 * CHUNK : (p + 1) * 4 * CHUNK, :]
        for q in range(4):
            span = slice(q * (D // 4), (q + 1) * (D // 4))
            found = jnp.dot(lhs, wv[:, span], preferred_element_type=F32).astype(BF16)
            pb[4 * p : 4 * p + 4, :, span] = found.reshape(4, CHUNK, D // 4)
    arrived()

    text_parts = [
        remote(tp.at[k], trb.at[mine], tss.at[k], trs.at[mine], gatherer(k)) for k in range(4)
    ]
    own_part = pltpu.make_async_copy(tp.at[0], trb.at[mine], trs.at[mine])

    @pl.when(own_piece)
    def _():
        own_part.start()

    @pl.when(jnp.logical_not(own_piece))
    def _():
        text_parts[0].start()

    for text_part in text_parts[1:]:
        text_part.start()
    far_device = me.at(y=lax.rem(me.y + 3 + 2 * c, 4))
    near_device = far_device
    near_slot = 3 - 2 * c
    plain_device = me.at(y=lax.rem(me.y + 1 + 2 * c, 4))
    plain_slot = 1 + 2 * c

    def far_copy(p):
        return remote(pb.at[4 * p + 2], fb.at[p], fs.at[p], fr.at[p], far_device)

    def plain_copy(p):
        return remote(pb.at[4 * p + plain_slot], nb.at[p, 0], ns.at[p, 0], nr.at[p, 0], plain_device)

    def sum_copy(p):
        return remote(pb.at[4 * p + near_slot], nb.at[p, 1], ns.at[p, 1], nr.at[p, 1], near_device)

    for p in (1, 0):
        far_copy(p).start()
        plain_copy(p).start()

    def relay(p):
        far_copy(p).wait_recv()
        total = pb[4 * p + near_slot].astype(F32) + fb[p].astype(F32)
        pb[4 * p + near_slot] = total.astype(BF16)
        sum_copy(p).start()

    def collect(p):
        plain_copy(p).wait_recv()
        sum_copy(p).wait_recv()
        return pb[4 * p].astype(F32) + nb[p, 0].astype(F32) + nb[p, 1].astype(F32)

    mirror = remote(zs, zb, zsem, zr, me.group(0, 1))
    relay(1)
    zs[...] = collect(1).astype(BF16)
    mirror.start()

    shares = [
        remote(tfin, tall.at[me.x, half, c], bs.at[i], br.at[half, c], device)
        for i, device in enumerate(column[1:])
    ]

    @pl.when(home)
    def _():
        total = jnp.zeros((TXT, D // 8), F32)
        for s in range(8):
            pltpu.make_async_copy(trb.at[s], trb.at[s], trs.at[s]).wait()
            total = total + trb[s].astype(F32)
        width = D // 8
        at = pl.ds(pl.multiple_of(c * half_cols + me.x * width, width), width)
        tfin[...] = (total * mt[2:3, at].astype(F32)).astype(BF16)
        for share in shares:
            share.start()
        tall[me.x, half, c] = tfin[...]

    relay(0)
    for b in range(2):
        for r in range(2):
            @pl.when(jnp.logical_not(jnp.logical_and(home, jnp.logical_and(half == b, c == r))))
            def _():
                dst = tall.at[me.x, b, r]
                pltpu.make_async_copy(dst, dst, br.at[b, r]).wait()

    spreads = [
        remote(tall.at[me.x], tall.at[me.x], xs.at[d], xr.at[d], device)
        for d, device in enumerate(across)
    ]
    for copy in spreads:
        copy.start()
    summed = collect(0)
    mirror.wait_recv()
    summed = summed + zb[...].astype(F32)
    video_out[...] = (summed * mv[2:3].astype(F32)).astype(BF16)

    for copy in spreads:
        copy.wait_recv()
    for k in range(4):
        for b in range(2):
            for r in range(2):
                at = r * half_cols + k * (D // 8)
                text_out[b * TXT : (b + 1) * TXT, at : at + D // 8] = tall[k, b, r]
    for p in (0, 1):
        far_copy(p).wait_send()
        plain_copy(p).wait_send()
        sum_copy(p).wait_send()
    mirror.wait_send()

    @pl.when(jnp.logical_not(own_piece))
    def _():
        text_parts[0].wait_send()

    for copy in text_parts[1:] + spreads:
        copy.wait_send()

    @pl.when(home)
    def _():
        for share in shares:
            share.wait_send()


def finish(heads, theads, mv, mt, wv, wt):
    half_cols = D // 2
    return pl.pallas_call(
        finish_kernel,
        out_shape=(
            jax.ShapeDtypeStruct((CHUNK, D), BF16),
            jax.ShapeDtypeStruct((2 * TXT, D), BF16),
        ),
        in_specs=vmem(4) + hbm(2),
        out_specs=tuple(vmem(2)),
        scratch_shapes=[
            pltpu.VMEM((8, CHUNK, D), BF16),
            pltpu.VMEM((2, CHUNK, D), BF16),
            pltpu.VMEM((2, 2, CHUNK, D), BF16),
            pltpu.VMEM((CHUNK, D), BF16),
            pltpu.VMEM((CHUNK, D), BF16),
            pltpu.VMEM((4, TXT, D // 8), BF16),
            pltpu.VMEM((8, TXT, D // 8), BF16),
            pltpu.VMEM((TXT, D // 8), BF16),
            pltpu.VMEM((4, 2, 2, TXT, D // 8), BF16),
            pltpu.VMEM((2 * HD, D), BF16),
            pltpu.VMEM((2 * HD, half_cols), BF16),
            DMA((2,)), DMA((2,)), DMA((2,)), DMA((2, 2)), DMA((2, 2)), DMA, DMA,
            DMA((4,)), DMA((8,)), DMA((7,)), DMA((2, 2)), DMA((3,)), DMA((3,)),
        ],
        compiler_params=pltpu.CompilerParams(collective_id=2, has_side_effects=True),
        name="finish",
    )(heads, theads, mv, mt, wv, wt)


def local(
    video_tokens, text_tokens, video_modulation, text_modulation, video_projection,
    text_projection, video_output, text_output, video_gains, text_gains,
):
    qkv, tqkv = project(
        video_tokens, text_tokens, video_modulation, text_modulation, video_gains, text_gains,
        jnp.transpose(video_projection, (1, 0, 2)), jnp.transpose(text_projection, (1, 0, 2)),
    )
    heads, theads = attend(qkv, tqkv)
    return finish(heads, theads, video_modulation, text_modulation, video_output, text_output)


def solution(mesh):
    torus = Mesh(mesh.devices.reshape(4, 4, 2, 4, 2), AX)
    placed = (
        P(AX, None),
        P(ULY, None),
        P(),
        P(),
        P(None, None, ULY),
        P(None, None, ULY),
        P(ULY, None),
        P(ULY, None),
        P(),
        P(),
    )
    return jax.shard_map(
        local,
        mesh=torus,
        in_specs=placed,
        out_specs=(P(AX, None), P(ULY, None)),
        check_vma=False,
    )
```

```python
import math

import jax
import jax.numpy as jnp
from jax import lax
from jax.experimental import pallas as pl
from jax.experimental.pallas import tpu as pltpu
from jax.sharding import Mesh
from jax.sharding import PartitionSpec as P

D = 3072
HD = 128
EPS = 1e-06
MESH = pl.DeviceIdType.MESH
AX = ("x", "zl", "c", "y", "zh")
ULY = ("y", "zh")
CHUNK = 48
ROWS = 8 * CHUNK
TXT = 16
LOG2 = math.log2(math.e) / math.sqrt(HD)
F32 = jnp.float32
BF16 = jnp.bfloat16


class Place:
    def __init__(self):
        self.x, self.zl, self.c, self.y, self.zh = (lax.axis_index(a) for a in AX)

    def at(self, **moved):
        found = {"x": self.x, "zl": self.zl, "c": self.c, "y": self.y, "zh": self.zh}
        found.update(moved)
        return found

    def group(self, dy, dz):
        y = lax.rem(self.y + dy, 4)
        if dz:
            return self.at(y=y, zh=1 - self.zh, zl=3 - self.zl)
        return self.at(y=y)

    def piece(self):
        return lax.rem(self.y + self.x, 4), jnp.where(self.zl < 2, self.zh, 1 - self.zh), lax.rem(self.zl, 2)


GROUP = [(dy, dz) for dz in (0, 1) for dy in range(4) if (dy, dz) != (0, 0)]


def greet(devices, more=0):
    barrier = pltpu.get_barrier_semaphore()
    for device in devices:
        pl.semaphore_signal(barrier, inc=1, device_id=device, device_id_type=MESH)
    return lambda: pl.semaphore_wait(barrier, len(devices) + more)


def remote(src, dst, ssem, rsem, device):
    return pltpu.make_async_remote_copy(
        src_ref=src, dst_ref=dst, send_sem=ssem, recv_sem=rsem,
        device_id=device, device_id_type=MESH,
    )


def modulate(rows, factors):
    floats = rows.astype(F32)
    centre = floats - jnp.mean(floats, axis=-1, keepdims=True)
    spread = jnp.mean(centre * centre, axis=-1, keepdims=True)
    normed = centre / jnp.sqrt(spread + EPS)
    return (normed * (1.0 + factors[1:2].astype(F32)) + factors[0:1].astype(F32)).astype(BF16)


def head_norm(vectors, gain):
    inverse = lax.rsqrt(jnp.mean(vectors * vectors, axis=-1, keepdims=True) + EPS)
    return (vectors * inverse * gain).astype(BF16)


HALF = ROWS // 2
SLOT = 2 * HALF
SPAN = 4 * SLOT


def mix_kernel(
    xv, xt, mv, mt, gv, gt, wv_hbm, wt_hbm, heads, theads,
    rows, ttmp, trow, wv, wt, qkv, tqkv, qb, kva, kvb, tq, mb, lb, ab,
    ob, sb, tob, orecv, srecv, trecv,
    wsem, gs, gr, tgs, tgr,
    kvs, kvr, qs, qr, tks, tkr, tqs, tqr, os_, or_, ss, sr, ts, tr,
):
    me = Place()
    c = me.c
    other = 1 - c
    load_v = pltpu.make_async_copy(wv_hbm, wv, wsem.at[0])
    load_t = pltpu.make_async_copy(
        wt_hbm.at[:, :, pl.ds(pl.multiple_of(c * HD, HD), HD)], wt, wsem.at[1]
    )
    load_v.start()
    load_t.start()
    peers = [me.group(dy, dz) for dy, dz in GROUP] + [me.at(c=other)]
    for d in range(1, 4):
        for r in (c, other):
            peers.append(me.at(x=lax.rem(me.x + d, 4), c=r))
            peers.append(me.at(zl=lax.rem(me.zl + d, 4), c=r))
    arrived = greet(peers)
    rows[0] = modulate(xv[...], mv[...])
    low_chip = me.zl < 2
    stays = jnp.logical_and(low_chip, me.x == 0)

    @pl.when(low_chip)
    def _():
        for b in range(2):
            ttmp[b] = modulate(xt[b * TXT : (b + 1) * TXT, :], mt[...])

    @pl.when(stays)
    def _():
        trow[...] = ttmp[me.zl]

    arrived()


    def copy_rows(src, dst, device):
        return remote(rows.at[src], rows.at[dst], gs.at[dst], gr.at[dst], device)

    up, down = me.group(1, 0), me.group(3, 0)
    far_src = 3 - 2 * c
    far_device = me.at(y=lax.rem(me.y + 1 + 2 * c, 4))

    mirror = copy_rows(0, 4, me.group(0, 1))
    mirror.start()

    def spread(base):
        low, high = copy_rows(base, base + 1, down), copy_rows(base, base + 3, up)

        @pl.when(c == 0)
        def _():
            high.start()
            low.start()

        @pl.when(c == 1)
        def _():
            low.start()
            high.start()

        return low, high

    def onward(base, low, high):
        far = copy_rows(base + far_src, base + 2, far_device)

        @pl.when(c == 0)
        def _():
            high.wait_recv()
            far.start()
            low.wait_recv()

        @pl.when(c == 1)
        def _():
            low.wait_recv()
            far.start()
            high.wait_recv()

        return far

    text_y = lax.rem(me.y + 4 - me.x, 4)
    text_near = remote(ttmp.at[lax.rem(me.zl, 2)], trow, tgs.at[0], tgr, me.at(y=text_y))
    text_over = remote(
        ttmp.at[1 - lax.rem(me.zl, 2)], trow, tgs.at[1], tgr,
        me.at(y=text_y, zh=1 - me.zh, zl=3 - me.zl),
    )

    def block(p):
        lhs = rows[4 * p : 4 * p + 4].reshape(HALF, D)
        for j in range(3):
            total = jnp.dot(lhs, wv[j], preferred_element_type=F32)
            for h in range(2):
                part = total[:, h * HD : (h + 1) * HD]
                part = head_norm(part, gv[j : j + 1]) if j < 2 else part.astype(BF16)
                qkv[h, p, j] = part


    sends = []

    def send(copy):
        copy.start()
        sends.append(copy)

    def kv_rows(p, slot, core):
        at = pl.ds(pl.multiple_of(slot * SLOT + core * HALF, HALF), HALF)
        return (kvb if p else kva).at[:, at, :]

    def q_rows(p, slot, core):
        return qb.at[p, slot, pl.ds(pl.multiple_of(core * HALF, HALF), HALF), :]

    def kv_text(slot):
        return kvb.at[:, pl.ds(SPAN + TXT * slot, TXT), :]

    def q_text(slot):
        return tq.at[pl.ds(TXT * slot, TXT), :]

    def along(axis, d, r):
        return me.at(**{axis: lax.rem(getattr(me, axis) + d, 4), "c": r})

    def exchange(p):
        pltpu.make_async_copy(qkv.at[c, p, 0], q_rows(p, 0, c), qr.at[p, 0, 0]).start()
        pltpu.make_async_copy(
            qkv.at[c, p, pl.ds(1, 2)], kv_rows(p, 0, c), kvr.at[p, 0, 0]
        ).start()
        for d in (0, 3, 1, 2):
            slot = (4 - d) % 4
            for i, r in enumerate((c, other)):
                if d or i:
                    send(remote(
                        qkv.at[r, p, 0], q_rows(p, slot, c),
                        qs.at[p, slot, i], qr.at[p, slot, i], along("zl", d, r),
                    ))
            for i, r in enumerate((c, other)):
                if d or i:
                    send(remote(
                        qkv.at[r, p, pl.ds(1, 2)], kv_rows(p, slot, c),
                        kvs.at[p, slot, i], kvr.at[p, slot, i], along("x", d, r),
                    ))

    def exchange_text():
        pltpu.make_async_copy(tqkv.at[0], q_text(0), tqr.at[0]).start()
        pltpu.make_async_copy(tqkv.at[pl.ds(1, 2)], kv_text(0), tkr.at[0]).start()
        for d in (3, 1, 2):
            slot = (4 - d) % 4
            send(remote(tqkv.at[0], q_text(slot), tqs.at[slot], tqr.at[slot], along("zl", d, c)))
            send(remote(
                tqkv.at[pl.ds(1, 2)], kv_text(slot), tks.at[slot], tkr.at[slot], along("x", d, c)
            ))

    def landed(dst, sem):
        pltpu.make_async_copy(dst, dst, sem).wait()

    def await_kv(p):
        for slot in (0, 1, 3, 2):
            for i in range(2):
                landed(kv_rows(p, slot, i), kvr.at[p, slot, i])

    def await_q(p, slot):
        for i in range(2):
            landed(q_rows(p, slot, i), qr.at[p, slot, i])

    def scored(queries, keys):
        return lax.dot_general(
            queries, keys, (((1,), (1,)), ((), ())), preferred_element_type=F32
        )

    def lanes(weights):
        width = weights.shape[1]
        if width % HD:
            extra = weights[:, width - width % HD :]
            pad = jnp.zeros((extra.shape[0], HD - width % HD), F32)
            total = jnp.concatenate([extra, pad], axis=1)
        else:
            total = jnp.zeros((weights.shape[0], HD), F32)
        for k in range(width // HD):
            total = total + weights[:, k * HD : (k + 1) * HD]
        return total

    def open_step(queries, at):
        scores = scored(queries, kva[0])
        now = jnp.max(scores, axis=-1, keepdims=True)
        weights = jnp.exp2((scores - now) * LOG2)
        mb[at, :] = jnp.broadcast_to(now, (queries.shape[0], HD))
        lb[at, :] = lanes(weights)
        ab[at, :] = jnp.dot(weights.astype(BF16), kva[1], preferred_element_type=F32)

    def last_step(queries, at):
        scores = scored(queries, kvb[0])
        before = mb[at, :]
        now = jnp.maximum(before[:, :1], jnp.max(scores, axis=-1, keepdims=True))
        weights = jnp.exp2((scores - now) * LOG2)
        shrink = jnp.exp2((before - now) * LOG2)
        totals = jnp.sum(lb[at, :] * shrink + lanes(weights), axis=-1, keepdims=True)
        sums = ab[at, :] * shrink + jnp.dot(
            weights.astype(BF16), kvb[1], preferred_element_type=F32
        )
        level = jnp.broadcast_to(now * LOG2 + jnp.log2(totals), sums.shape)
        return sums / totals, level

    tail = pl.ds(2 * SPAN, 4 * TXT)

    def state_rows(p, slot):
        return pl.ds(pl.multiple_of((p * 4 + slot) * SLOT, SLOT), SLOT)

    def open_phase(p):
        def pair(i, _):
            slots = (3 * i, 1 + i)
            for slot in slots:
                await_q(p, slot)
            for slot in slots:
                open_step(qb[p, slot], state_rows(p, slot))
            return 0

        lax.fori_loop(0, 2, pair, 0)

    def out_copies(p, j, slot, i, r):
        device = along("zl", j, r)
        return (
            remote(
                ob.at[p, j, pl.ds(pl.multiple_of(r * HALF, HALF), HALF), :], orecv.at[p, slot, c],
                os_.at[p, slot, i], or_.at[p, slot, i], device,
            ),
            remote(
                sb.at[p, j, r], srecv.at[p, slot, c], ss.at[p, slot, i], sr.at[p, slot, i], device
            ),
        )

    def last_phase(p):
        def pair(n, _):
            slots = (2 - 2 * n, 3 - 2 * n)
            for slot in slots:
                mixed, level = last_step(qb[p, slot], state_rows(p, slot))
                ob[p, slot] = mixed.astype(BF16)
                for r in range(2):
                    part = level[r * HALF : (r + 1) * HALF]
                    sb[p, slot, r] = jnp.transpose(part)[:8, :]

            @pl.when(n == 0)
            def _():
                for j in (2, 3):
                    for i, r in enumerate((c, other)):
                        for copy in out_copies(p, j, 4 - j, i, r):
                            copy.start()

            @pl.when(n == 1)
            def _():
                for i, r in enumerate((c, other)):
                    for copy in out_copies(p, 1, 3, i, r):
                        copy.start()
                for copy in out_copies(p, 0, 0, 1, other):
                    copy.start()
                at = pl.ds(pl.multiple_of(c * HALF, HALF), HALF)
                pltpu.make_async_copy(
                    ob.at[p, 0, at, :], orecv.at[p, 0, c], or_.at[p, 0, 0]
                ).start()
                pltpu.make_async_copy(sb.at[p, 0, c], srecv.at[p, 0, c], sr.at[p, 0, 0]).start()

            return 0

        lax.fori_loop(0, 2, pair, 0)

    def merge(p):
        for slot in range(4):
            for i, r in enumerate((c, other)):
                landed(orecv.at[p, slot, r], or_.at[p, slot, i])
                landed(srecv.at[p, slot, r], sr.at[p, slot, i])
        for h in range(2):
            found = [srecv[p, slot, h] for slot in range(4)]
            top = jnp.maximum(jnp.maximum(found[0], found[1]), jnp.maximum(found[2], found[3]))
            weight = [jnp.exp2(part - top) for part in found]
            share = 1.0 / sum(weight)
            mixed = jnp.zeros((HALF, HD), F32)
            for slot in range(4):
                row = (weight[slot] * share)[:1]
                column = jnp.transpose(jnp.broadcast_to(row, (HD, HALF)))
                mixed = mixed + column * orecv[p, slot, h].astype(F32)
            heads[p * HALF : (p + 1) * HALF, h * HD : (h + 1) * HD] = mixed.astype(BF16)

    def send_text():
        mixed, level = last_step(tq[...], tail)
        tob[:, :HD] = mixed
        tob[:, HD:] = level
        for j in range(4):
            slot = (4 - j) % 4
            for i, r in enumerate((c, other)):
                src, dst = tob.at[pl.ds(TXT * j, TXT), :], trecv.at[slot, c]
                if j == 0 and i == 0:
                    pltpu.make_async_copy(src, dst, tr.at[0, 0]).start()
                else:
                    send(remote(src, dst, ts.at[slot, i], tr.at[slot, i], along("zl", j, r)))

    def merge_text():
        for slot in range(4):
            for i, r in enumerate((c, other)):
                landed(trecv.at[slot, r], tr.at[slot, i])
        for h in range(2):
            found = [trecv[slot, h] for slot in range(4)]
            top = found[0][:, HD:]
            for part in found[1:]:
                top = jnp.maximum(top, part[:, HD:])
            weight = [jnp.exp2(part[:, HD:] - top) for part in found]
            mixed = sum(w * part[:, :HD] for w, part in zip(weight, found)) / sum(weight)
            theads[:, h * HD : (h + 1) * HD] = mixed.astype(BF16)

    first = spread(0)

    @pl.when(low_chip)
    def _():
        text_over.start()

    @pl.when(jnp.logical_and(low_chip, me.x > 0))
    def _():
        text_near.start()

    far0 = onward(0, *first)
    mirror.wait_recv()
    second = spread(4)
    load_v.wait()
    far0.wait_recv()
    block(0)
    exchange(0)
    far1 = onward(4, *second)

    @pl.when(jnp.logical_not(stays))
    def _():
        text_near.wait_recv()

    load_t.wait()
    for j in range(3):
        part = jnp.dot(trow[...], wt[j], preferred_element_type=F32)
        tqkv[j] = head_norm(part, gt[j : j + 1]) if j < 2 else part.astype(BF16)
    exchange_text()
    await_kv(0)
    open_phase(0)
    far1.wait_recv()
    block(1)
    exchange(1)
    for j in range(4):
        landed(q_text(j), tqr.at[j])
    open_step(tq[...], tail)
    open_phase(1)
    await_kv(1)
    for j in range(4):
        landed(kv_text(j), tkr.at[j])
    send_text()
    last_phase(1)
    last_phase(0)
    merge_text()
    merge(1)
    merge(0)

    for copy in (mirror, *first, far0, *second, far1):
        copy.wait_send()

    @pl.when(low_chip)
    def _():
        text_over.wait_send()

    @pl.when(jnp.logical_and(low_chip, me.x > 0))
    def _():
        text_near.wait_send()

    for copy in sends:
        copy.wait_send()
    for p in range(2):
        for slot in range(4):
            for i, r in enumerate((c, other)):
                if (slot, i) != (0, 0):
                    for copy in out_copies(p, (4 - slot) % 4, slot, i, r):
                        copy.wait_send()


def vmem(n):
    return [pl.BlockSpec(memory_space=pltpu.VMEM)] * n


def hbm(n):
    return [pl.BlockSpec(memory_space=pl.ANY)] * n


DMA = pltpu.SemaphoreType.DMA


def mix(xv, xt, mv, mt, gv, gt, wv, wt):
    states = 2 * SPAN + 4 * TXT
    return pl.pallas_call(
        mix_kernel,
        out_shape=(
            jax.ShapeDtypeStruct((ROWS, 2 * HD), BF16),
            jax.ShapeDtypeStruct((TXT, 2 * HD), BF16),
        ),
        in_specs=vmem(6) + hbm(2),
        out_specs=tuple(vmem(2)),
        scratch_shapes=[
            pltpu.VMEM((8, CHUNK, D), BF16),
            pltpu.VMEM((2, TXT, D), BF16),
            pltpu.VMEM((TXT, D), BF16),
            pltpu.VMEM((3, D, 2 * HD), BF16),
            pltpu.VMEM((3, D, HD), BF16),
            pltpu.VMEM((2, 2, 3, HALF, HD), BF16),
            pltpu.VMEM((3, TXT, HD), BF16),
            pltpu.VMEM((2, 4, SLOT, HD), BF16),
            pltpu.VMEM((2, SPAN, HD), BF16),
            pltpu.VMEM((2, SPAN + 4 * TXT, HD), BF16),
            pltpu.VMEM((4 * TXT, HD), BF16),
            pltpu.VMEM((states, HD), F32),
            pltpu.VMEM((states, HD), F32),
            pltpu.VMEM((states, HD), F32),
            pltpu.VMEM((2, 4, SLOT, HD), BF16),
            pltpu.VMEM((2, 4, 2, 8, HALF), F32),
            pltpu.VMEM((4 * TXT, 2 * HD), F32),
            pltpu.VMEM((2, 4, 2, HALF, HD), BF16),
            pltpu.VMEM((2, 4, 2, 8, HALF), F32),
            pltpu.VMEM((4, 2, TXT, 2 * HD), F32),
            DMA((2,)), DMA((8,)), DMA((8,)), DMA((2,)), DMA,
        ]
        + [DMA((2, 4, 2))] * 4 + [DMA((4,))] * 4 + [DMA((2, 4, 2))] * 4 + [DMA((4, 2))] * 2,
        compiler_params=pltpu.CompilerParams(collective_id=0, has_side_effects=True),
        name="mix",
    )(xv, xt, mv, mt, gv, gt, wv, wt)


def finish_kernel(
    heads, theads, mv, mt, wv_hbm, wt_hbm, video_out, text_out,
    pb, fb, nb, zb, zs, tp, trb, tfin, tall, wv, wt,
    wsem, fs, fr, ns, nr, zsem, zr, tss, trs, bs, br, xs, xr,
):
    me = Place()
    c = me.c
    half_cols = D // 2
    load_v = pltpu.make_async_copy(wv_hbm, wv, wsem.at[0])
    cols = pl.ds(pl.multiple_of(c * half_cols, half_cols), half_cols)
    load_t = pltpu.make_async_copy(wt_hbm.at[:, cols], wt, wsem.at[1])
    load_v.start()
    load_t.start()
    piece_y, piece_zh, half = me.piece()
    mine = me.y * 2 + me.zh
    home = me.zl // 2 == c

    def gatherer(k):
        return me.at(x=k, zl=2 * c + half, y=piece_y, zh=piece_zh)

    def giver(s):
        y, zh = s // 2, s % 2
        side = jnp.where(me.zh == zh, 0, 1)
        return me.at(x=lax.rem(me.y + 4 - y, 4), zl=2 * side + half, y=y, zh=zh)

    own_piece = jnp.logical_and(me.x == 0, jnp.logical_and(me.zl < 2, c == 0))
    column = [me.at(zl=lax.rem(me.zl + d, 4), c=r) for d in range(4) for r in (c, 1 - c)]
    across = [me.at(x=lax.rem(me.x + d, 4)) for d in range(1, 4)]
    up, down = me.group(1, 0), me.group(3, 0)
    arrived = greet(
        [up, down, me.group(0, 1)] + column[1:] + across,
        4 - jnp.where(own_piece, 1, 0),
    )
    barrier = pltpu.get_barrier_semaphore()

    @pl.when(home)
    def _():
        for s in range(8):
            @pl.when(jnp.logical_not(jnp.logical_and(own_piece, s == mine)))
            def _():
                pl.semaphore_signal(barrier, inc=1, device_id=giver(s), device_id_type=MESH)

    load_t.wait()
    part = jnp.dot(theads[...], wt[...], preferred_element_type=F32).astype(BF16)
    for k in range(4):
        tp[k] = part[:, k * (D // 8) : (k + 1) * (D // 8)]
    load_v.wait()
    for p in (1, 0):
        lhs = heads[p * 4 * CHUNK : (p + 1) * 4 * CHUNK, :]
        for q in range(4):
            span = slice(q * (D // 4), (q + 1) * (D // 4))
            found = jnp.dot(lhs, wv[:, span], preferred_element_type=F32).astype(BF16)
            pb[4 * p : 4 * p + 4, :, span] = found.reshape(4, CHUNK, D // 4)
    arrived()

    text_parts = [
        remote(tp.at[k], trb.at[mine], tss.at[k], trs.at[mine], gatherer(k)) for k in range(4)
    ]
    own_part = pltpu.make_async_copy(tp.at[0], trb.at[mine], trs.at[mine])

    @pl.when(own_piece)
    def _():
        own_part.start()

    @pl.when(jnp.logical_not(own_piece))
    def _():
        text_parts[0].start()

    for text_part in text_parts[1:]:
        text_part.start()
    far_device = me.at(y=lax.rem(me.y + 3 + 2 * c, 4))
    near_device = far_device
    near_slot = 3 - 2 * c
    plain_device = me.at(y=lax.rem(me.y + 1 + 2 * c, 4))
    plain_slot = 1 + 2 * c

    def far_copy(p):
        return remote(pb.at[4 * p + 2], fb.at[p], fs.at[p], fr.at[p], far_device)

    def plain_copy(p):
        return remote(pb.at[4 * p + plain_slot], nb.at[p, 0], ns.at[p, 0], nr.at[p, 0], plain_device)

    def sum_copy(p):
        return remote(pb.at[4 * p + near_slot], nb.at[p, 1], ns.at[p, 1], nr.at[p, 1], near_device)

    for p in (1, 0):
        far_copy(p).start()
        plain_copy(p).start()

    def relay(p):
        far_copy(p).wait_recv()
        total = pb[4 * p + near_slot].astype(F32) + fb[p].astype(F32)
        pb[4 * p + near_slot] = total.astype(BF16)
        sum_copy(p).start()

    def collect(p):
        plain_copy(p).wait_recv()
        sum_copy(p).wait_recv()
        return pb[4 * p].astype(F32) + nb[p, 0].astype(F32) + nb[p, 1].astype(F32)

    mirror = remote(zs, zb, zsem, zr, me.group(0, 1))
    relay(1)
    zs[...] = collect(1).astype(BF16)
    mirror.start()

    shares = [
        remote(tfin, tall.at[me.x, half, c], bs.at[i], br.at[half, c], device)
        for i, device in enumerate(column[1:])
    ]

    @pl.when(home)
    def _():
        total = jnp.zeros((TXT, D // 8), F32)
        for s in range(8):
            pltpu.make_async_copy(trb.at[s], trb.at[s], trs.at[s]).wait()
            total = total + trb[s].astype(F32)
        width = D // 8
        at = pl.ds(pl.multiple_of(c * half_cols + me.x * width, width), width)
        tfin[...] = (total * mt[2:3, at].astype(F32)).astype(BF16)
        for share in shares:
            share.start()
        tall[me.x, half, c] = tfin[...]

    relay(0)
    for b in range(2):
        for r in range(2):
            @pl.when(jnp.logical_not(jnp.logical_and(home, jnp.logical_and(half == b, c == r))))
            def _():
                dst = tall.at[me.x, b, r]
                pltpu.make_async_copy(dst, dst, br.at[b, r]).wait()

    spreads = [
        remote(tall.at[me.x], tall.at[me.x], xs.at[d], xr.at[d], device)
        for d, device in enumerate(across)
    ]
    for copy in spreads:
        copy.start()
    summed = collect(0)
    mirror.wait_recv()
    summed = summed + zb[...].astype(F32)
    video_out[...] = (summed * mv[2:3].astype(F32)).astype(BF16)

    for copy in spreads:
        copy.wait_recv()
    for k in range(4):
        for b in range(2):
            for r in range(2):
                at = r * half_cols + k * (D // 8)
                text_out[b * TXT : (b + 1) * TXT, at : at + D // 8] = tall[k, b, r]
    for p in (0, 1):
        far_copy(p).wait_send()
        plain_copy(p).wait_send()
        sum_copy(p).wait_send()
    mirror.wait_send()

    @pl.when(jnp.logical_not(own_piece))
    def _():
        text_parts[0].wait_send()

    for copy in text_parts[1:] + spreads:
        copy.wait_send()

    @pl.when(home)
    def _():
        for share in shares:
            share.wait_send()


def finish(heads, theads, mv, mt, wv, wt):
    half_cols = D // 2
    return pl.pallas_call(
        finish_kernel,
        out_shape=(
            jax.ShapeDtypeStruct((CHUNK, D), BF16),
            jax.ShapeDtypeStruct((2 * TXT, D), BF16),
        ),
        in_specs=vmem(4) + hbm(2),
        out_specs=tuple(vmem(2)),
        scratch_shapes=[
            pltpu.VMEM((8, CHUNK, D), BF16),
            pltpu.VMEM((2, CHUNK, D), BF16),
            pltpu.VMEM((2, 2, CHUNK, D), BF16),
            pltpu.VMEM((CHUNK, D), BF16),
            pltpu.VMEM((CHUNK, D), BF16),
            pltpu.VMEM((4, TXT, D // 8), BF16),
            pltpu.VMEM((8, TXT, D // 8), BF16),
            pltpu.VMEM((TXT, D // 8), BF16),
            pltpu.VMEM((4, 2, 2, TXT, D // 8), BF16),
            pltpu.VMEM((2 * HD, D), BF16),
            pltpu.VMEM((2 * HD, half_cols), BF16),
            DMA((2,)), DMA((2,)), DMA((2,)), DMA((2, 2)), DMA((2, 2)), DMA, DMA,
            DMA((4,)), DMA((8,)), DMA((7,)), DMA((2, 2)), DMA((3,)), DMA((3,)),
        ],
        compiler_params=pltpu.CompilerParams(collective_id=1, has_side_effects=True),
        name="finish",
    )(heads, theads, mv, mt, wv, wt)


def local(
    video_tokens, text_tokens, video_modulation, text_modulation, video_projection,
    text_projection, video_output, text_output, video_gains, text_gains,
):
    heads, theads = mix(
        video_tokens, text_tokens, video_modulation, text_modulation, video_gains, text_gains,
        jnp.transpose(video_projection, (1, 0, 2)), jnp.transpose(text_projection, (1, 0, 2)),
    )
    return finish(heads, theads, video_modulation, text_modulation, video_output, text_output)


def solution(mesh):
    torus = Mesh(mesh.devices.reshape(4, 4, 2, 4, 2), AX)
    placed = (
        P(AX, None),
        P(ULY, None),
        P(),
        P(),
        P(None, None, ULY),
        P(None, None, ULY),
        P(ULY, None),
        P(ULY, None),
        P(),
        P(),
    )
    return jax.shard_map(
        local,
        mesh=torus,
        in_specs=placed,
        out_specs=(P(AX, None), P(ULY, None)),
        check_vma=False,
    )
```

```python
import math

import jax
import jax.numpy as jnp
from jax import lax
from jax.experimental import pallas as pl
from jax.experimental.pallas import tpu as pltpu
from jax.sharding import Mesh
from jax.sharding import PartitionSpec as P

D = 3072
HD = 128
EPS = 1e-06
MESH = pl.DeviceIdType.MESH
AX = ("x", "zl", "c", "y", "zh")
ULY = ("y", "zh")
CHUNK = 48
ROWS = 8 * CHUNK
TXT = 16
LOG2 = math.log2(math.e) / math.sqrt(HD)
F32 = jnp.float32
BF16 = jnp.bfloat16


class Place:
    def __init__(self):
        self.x, self.zl, self.c, self.y, self.zh = (lax.axis_index(a) for a in AX)

    def at(self, **moved):
        found = {"x": self.x, "zl": self.zl, "c": self.c, "y": self.y, "zh": self.zh}
        found.update(moved)
        return found

    def group(self, dy, dz):
        y = lax.rem(self.y + dy, 4)
        if dz:
            return self.at(y=y, zh=1 - self.zh, zl=3 - self.zl)
        return self.at(y=y)

    def piece(self):
        return lax.rem(self.y + self.x, 4), jnp.where(self.zl < 2, self.zh, 1 - self.zh), lax.rem(self.zl, 2)


GROUP = [(dy, dz) for dz in (0, 1) for dy in range(4) if (dy, dz) != (0, 0)]


def greet(devices, more=0):
    barrier = pltpu.get_barrier_semaphore()
    for device in devices:
        pl.semaphore_signal(barrier, inc=1, device_id=device, device_id_type=MESH)
    return lambda: pl.semaphore_wait(barrier, len(devices) + more)


def remote(src, dst, ssem, rsem, device):
    return pltpu.make_async_remote_copy(
        src_ref=src, dst_ref=dst, send_sem=ssem, recv_sem=rsem,
        device_id=device, device_id_type=MESH,
    )


def modulate(rows, factors):
    floats = rows.astype(F32)
    centre = floats - jnp.mean(floats, axis=-1, keepdims=True)
    spread = jnp.mean(centre * centre, axis=-1, keepdims=True)
    normed = centre / jnp.sqrt(spread + EPS)
    return (normed * (1.0 + factors[1:2].astype(F32)) + factors[0:1].astype(F32)).astype(BF16)


def head_norm(vectors, gain):
    inverse = lax.rsqrt(jnp.mean(vectors * vectors, axis=-1, keepdims=True) + EPS)
    return (vectors * inverse * gain).astype(BF16)


HALF = ROWS // 2
SLOT = 2 * HALF
SPAN = 4 * SLOT


def mix_kernel(
    xv, xt, mv, mt, gv, gt, wv_hbm, wt_hbm, heads, theads,
    rows, ttmp, trow, wv, wt, qkv, tqkv, qb, kva, kvb, tq, mb, lb, ab,
    ob, sb, tob, orecv, srecv, trecv,
    wsem, gs, gr, tgs, tgr,
    kvs, kvr, qs, qr, tks, tkr, tqs, tqr, os_, or_, ss, sr, ts, tr,
):
    me = Place()
    c = me.c
    other = 1 - c
    load_v = pltpu.make_async_copy(wv_hbm, wv, wsem.at[0])
    load_t = pltpu.make_async_copy(
        wt_hbm.at[:, :, pl.ds(pl.multiple_of(c * HD, HD), HD)], wt, wsem.at[1]
    )
    load_v.start()
    load_t.start()
    peers = [me.group(dy, dz) for dy, dz in GROUP] + [me.at(c=other)]
    for d in range(1, 4):
        for r in (c, other):
            peers.append(me.at(x=lax.rem(me.x + d, 4), c=r))
            peers.append(me.at(zl=lax.rem(me.zl + d, 4), c=r))
    arrived = greet(peers)
    rows[0] = modulate(xv[...], mv[...])
    low_chip = me.zl < 2
    stays = jnp.logical_and(low_chip, me.x == 0)

    @pl.when(low_chip)
    def _():
        for b in range(2):
            ttmp[b] = modulate(xt[b * TXT : (b + 1) * TXT, :], mt[...])

    @pl.when(stays)
    def _():
        trow[...] = ttmp[me.zl]

    arrived()


    def copy_rows(src, dst, device):
        return [
            remote(
                rows.at[src, :, pl.ds(h * (D // 2), D // 2)], rows.at[dst, :, pl.ds(h * (D // 2), D // 2)],
                gs.at[dst, h], gr.at[dst, h], device,
            )
            for h in range(2)
        ]

    up, down = me.group(1, 0), me.group(3, 0)
    far_src = 3 - 2 * c
    far_device = me.at(y=lax.rem(me.y + 1 + 2 * c, 4))
    mirror = copy_rows(0, 4, me.group(0, 1))
    moves = [
        (copy_rows(b, b + 1, down), copy_rows(b, b + 3, up), copy_rows(b + far_src, b + 2, far_device))
        for b in (0, 4)
    ]

    def spread(p, h):
        low, high, _ = moves[p]
        high[h].start()
        low[h].start()

    def onward(p, h):
        low, high, far = moves[p]

        @pl.when(c == 0)
        def _():
            high[h].wait_recv()

        @pl.when(c == 1)
        def _():
            low[h].wait_recv()

        far[h].start()

    def gathered(p):
        low, high, far = moves[p]

        @pl.when(c == 0)
        def _():
            for copy in low:
                copy.wait_recv()

        @pl.when(c == 1)
        def _():
            for copy in high:
                copy.wait_recv()

        for copy in far:
            copy.wait_recv()

    text_y = lax.rem(me.y + 4 - me.x, 4)
    text_near = remote(ttmp.at[lax.rem(me.zl, 2)], trow, tgs.at[0], tgr, me.at(y=text_y))
    text_over = remote(
        ttmp.at[1 - lax.rem(me.zl, 2)], trow, tgs.at[1], tgr,
        me.at(y=text_y, zh=1 - me.zh, zl=3 - me.zl),
    )

    def block(p):
        lhs = rows[4 * p : 4 * p + 4].reshape(HALF, D)
        for j in range(3):
            total = jnp.dot(lhs, wv[j], preferred_element_type=F32)
            for h in range(2):
                part = total[:, h * HD : (h + 1) * HD]
                part = head_norm(part, gv[j : j + 1]) if j < 2 else part.astype(BF16)
                qkv[h, p, j] = part


    sends = []

    def send(copy):
        copy.start()
        sends.append(copy)

    def kv_rows(p, slot, core):
        at = pl.ds(pl.multiple_of(slot * SLOT + core * HALF, HALF), HALF)
        return (kvb if p else kva).at[:, at, :]

    def q_rows(p, slot, core):
        return qb.at[p, slot, pl.ds(pl.multiple_of(core * HALF, HALF), HALF), :]

    def kv_text(slot):
        return kvb.at[:, pl.ds(SPAN + TXT * slot, TXT), :]

    def q_text(slot):
        return tq.at[pl.ds(TXT * slot, TXT), :]

    def along(axis, d, r):
        return me.at(**{axis: lax.rem(getattr(me, axis) + d, 4), "c": r})

    def exchange(p):
        pltpu.make_async_copy(qkv.at[c, p, 0], q_rows(p, 0, c), qr.at[p, 0, 0]).start()
        pltpu.make_async_copy(
            qkv.at[c, p, pl.ds(1, 2)], kv_rows(p, 0, c), kvr.at[p, 0, 0]
        ).start()
        for d in (0, 3, 1, 2):
            slot = (4 - d) % 4
            for i, r in enumerate((c, other)):
                if d or i:
                    send(remote(
                        qkv.at[r, p, 0], q_rows(p, slot, c),
                        qs.at[p, slot, i], qr.at[p, slot, i], along("x", d, r),
                    ))
            for i, r in enumerate((c, other)):
                if d or i:
                    send(remote(
                        qkv.at[r, p, pl.ds(1, 2)], kv_rows(p, slot, c),
                        kvs.at[p, slot, i], kvr.at[p, slot, i], along("zl", d, r),
                    ))

    def exchange_text():
        pltpu.make_async_copy(tqkv.at[0], q_text(0), tqr.at[0]).start()
        pltpu.make_async_copy(tqkv.at[pl.ds(1, 2)], kv_text(0), tkr.at[0]).start()
        for d in (3, 1, 2):
            slot = (4 - d) % 4
            send(remote(tqkv.at[0], q_text(slot), tqs.at[slot], tqr.at[slot], along("x", d, c)))
            send(remote(
                tqkv.at[pl.ds(1, 2)], kv_text(slot), tks.at[slot], tkr.at[slot], along("zl", d, c)
            ))

    def landed(dst, sem):
        pltpu.make_async_copy(dst, dst, sem).wait()

    def await_kv(p):
        for slot in (0, 1, 3, 2):
            for i in range(2):
                landed(kv_rows(p, slot, i), kvr.at[p, slot, i])

    def await_q(p, slot):
        for i in range(2):
            landed(q_rows(p, slot, i), qr.at[p, slot, i])

    def scored(queries, keys):
        return lax.dot_general(
            queries, keys, (((1,), (1,)), ((), ())), preferred_element_type=F32
        )

    def lanes(weights):
        width = weights.shape[1]
        if width % HD:
            extra = weights[:, width - width % HD :]
            pad = jnp.zeros((extra.shape[0], HD - width % HD), F32)
            total = jnp.concatenate([extra, pad], axis=1)
        else:
            total = jnp.zeros((weights.shape[0], HD), F32)
        for k in range(width // HD):
            total = total + weights[:, k * HD : (k + 1) * HD]
        return total

    def open_step(queries, at):
        scores = scored(queries, kva[0])
        now = jnp.max(scores, axis=-1, keepdims=True)
        weights = jnp.exp2((scores - now) * LOG2)
        mb[at, :] = jnp.broadcast_to(now, (queries.shape[0], HD))
        lb[at, :] = lanes(weights)
        ab[at, :] = jnp.dot(weights.astype(BF16), kva[1], preferred_element_type=F32)

    def last_step(queries, at):
        scores = scored(queries, kvb[0])
        before = mb[at, :]
        now = jnp.maximum(before[:, :1], jnp.max(scores, axis=-1, keepdims=True))
        weights = jnp.exp2((scores - now) * LOG2)
        shrink = jnp.exp2((before - now) * LOG2)
        totals = jnp.sum(lb[at, :] * shrink + lanes(weights), axis=-1, keepdims=True)
        sums = ab[at, :] * shrink + jnp.dot(
            weights.astype(BF16), kvb[1], preferred_element_type=F32
        )
        level = jnp.broadcast_to(now * LOG2 + jnp.log2(totals), sums.shape)
        return sums / totals, level

    tail = pl.ds(2 * SPAN, 4 * TXT)

    def state_rows(p, slot):
        return pl.ds(pl.multiple_of((p * 4 + slot) * SLOT, SLOT), SLOT)

    def open_phase(p):
        def pair(i, _):
            slots = (3 * i, 1 + i)
            for slot in slots:
                await_q(p, slot)
            for slot in slots:
                open_step(qb[p, slot], state_rows(p, slot))
            return 0

        lax.fori_loop(0, 2, pair, 0)

    def out_copies(p, j, slot, i, r):
        device = along("x", j, r)
        return (
            remote(
                ob.at[p, j, pl.ds(pl.multiple_of(r * HALF, HALF), HALF), :], orecv.at[p, slot, c],
                os_.at[p, slot, i], or_.at[p, slot, i], device,
            ),
            remote(
                sb.at[p, j, r], srecv.at[p, slot, c], ss.at[p, slot, i], sr.at[p, slot, i], device
            ),
        )

    def last_phase(p):
        def pair(n, _):
            slots = (2 - 2 * n, 3 - 2 * n)
            for slot in slots:
                mixed, level = last_step(qb[p, slot], state_rows(p, slot))
                ob[p, slot] = mixed.astype(BF16)
                for r in range(2):
                    part = level[r * HALF : (r + 1) * HALF]
                    sb[p, slot, r] = jnp.transpose(part)[:8, :]

            @pl.when(n == 0)
            def _():
                for j in (2, 3):
                    for i, r in enumerate((c, other)):
                        for copy in out_copies(p, j, 4 - j, i, r):
                            copy.start()

            @pl.when(n == 1)
            def _():
                for i, r in enumerate((c, other)):
                    for copy in out_copies(p, 1, 3, i, r):
                        copy.start()
                for copy in out_copies(p, 0, 0, 1, other):
                    copy.start()
                at = pl.ds(pl.multiple_of(c * HALF, HALF), HALF)
                pltpu.make_async_copy(
                    ob.at[p, 0, at, :], orecv.at[p, 0, c], or_.at[p, 0, 0]
                ).start()
                pltpu.make_async_copy(sb.at[p, 0, c], srecv.at[p, 0, c], sr.at[p, 0, 0]).start()

            return 0

        lax.fori_loop(0, 2, pair, 0)

    def merge(p):
        for slot in range(4):
            for i, r in enumerate((c, other)):
                landed(orecv.at[p, slot, r], or_.at[p, slot, i])
                landed(srecv.at[p, slot, r], sr.at[p, slot, i])
        for h in range(2):
            found = [srecv[p, slot, h] for slot in range(4)]
            top = jnp.maximum(jnp.maximum(found[0], found[1]), jnp.maximum(found[2], found[3]))
            weight = [jnp.exp2(part - top) for part in found]
            share = 1.0 / sum(weight)
            mixed = jnp.zeros((HALF, HD), F32)
            for slot in range(4):
                row = (weight[slot] * share)[:1]
                column = jnp.transpose(jnp.broadcast_to(row, (HD, HALF)))
                mixed = mixed + column * orecv[p, slot, h].astype(F32)
            heads[p * HALF : (p + 1) * HALF, h * HD : (h + 1) * HD] = mixed.astype(BF16)

    def send_text():
        mixed, level = last_step(tq[...], tail)
        tob[:, :HD] = mixed
        tob[:, HD:] = level
        for j in range(4):
            slot = (4 - j) % 4
            for i, r in enumerate((c, other)):
                src, dst = tob.at[pl.ds(TXT * j, TXT), :], trecv.at[slot, c]
                if j == 0 and i == 0:
                    pltpu.make_async_copy(src, dst, tr.at[0, 0]).start()
                else:
                    send(remote(src, dst, ts.at[slot, i], tr.at[slot, i], along("x", j, r)))

    def merge_text():
        for slot in range(4):
            for i, r in enumerate((c, other)):
                landed(trecv.at[slot, r], tr.at[slot, i])
        for h in range(2):
            found = [trecv[slot, h] for slot in range(4)]
            top = found[0][:, HD:]
            for part in found[1:]:
                top = jnp.maximum(top, part[:, HD:])
            weight = [jnp.exp2(part[:, HD:] - top) for part in found]
            mixed = sum(w * part[:, :HD] for w, part in zip(weight, found)) / sum(weight)
            theads[:, h * HD : (h + 1) * HD] = mixed.astype(BF16)

    mirror[0].start()
    spread(0, 0)
    mirror[1].start()
    spread(0, 1)

    @pl.when(low_chip)
    def _():
        text_over.start()

    @pl.when(jnp.logical_and(low_chip, me.x > 0))
    def _():
        text_near.start()

    onward(0, 0)
    onward(0, 1)
    for h in range(2):
        mirror[h].wait_recv()
        spread(1, h)
    load_v.wait()
    gathered(0)
    block(0)
    exchange(0)
    onward(1, 0)
    onward(1, 1)

    @pl.when(jnp.logical_not(stays))
    def _():
        text_near.wait_recv()

    load_t.wait()
    for j in range(3):
        part = jnp.dot(trow[...], wt[j], preferred_element_type=F32)
        tqkv[j] = head_norm(part, gt[j : j + 1]) if j < 2 else part.astype(BF16)
    exchange_text()
    await_kv(0)
    open_phase(0)
    gathered(1)
    block(1)
    exchange(1)
    for j in range(4):
        landed(q_text(j), tqr.at[j])
    open_step(tq[...], tail)
    open_phase(1)
    await_kv(1)
    for j in range(4):
        landed(kv_text(j), tkr.at[j])
    send_text()
    last_phase(1)
    last_phase(0)
    merge_text()
    merge(1)
    merge(0)

    for pair in [mirror] + [found for move in moves for found in move]:
        for copy in pair:
            copy.wait_send()

    @pl.when(low_chip)
    def _():
        text_over.wait_send()

    @pl.when(jnp.logical_and(low_chip, me.x > 0))
    def _():
        text_near.wait_send()

    for copy in sends:
        copy.wait_send()
    for p in range(2):
        for slot in range(4):
            for i, r in enumerate((c, other)):
                if (slot, i) != (0, 0):
                    for copy in out_copies(p, (4 - slot) % 4, slot, i, r):
                        copy.wait_send()


def vmem(n):
    return [pl.BlockSpec(memory_space=pltpu.VMEM)] * n


def hbm(n):
    return [pl.BlockSpec(memory_space=pl.ANY)] * n


DMA = pltpu.SemaphoreType.DMA


def mix(xv, xt, mv, mt, gv, gt, wv, wt):
    states = 2 * SPAN + 4 * TXT
    return pl.pallas_call(
        mix_kernel,
        out_shape=(
            jax.ShapeDtypeStruct((ROWS, 2 * HD), BF16),
            jax.ShapeDtypeStruct((TXT, 2 * HD), BF16),
        ),
        in_specs=vmem(6) + hbm(2),
        out_specs=tuple(vmem(2)),
        scratch_shapes=[
            pltpu.VMEM((8, CHUNK, D), BF16),
            pltpu.VMEM((2, TXT, D), BF16),
            pltpu.VMEM((TXT, D), BF16),
            pltpu.VMEM((3, D, 2 * HD), BF16),
            pltpu.VMEM((3, D, HD), BF16),
            pltpu.VMEM((2, 2, 3, HALF, HD), BF16),
            pltpu.VMEM((3, TXT, HD), BF16),
            pltpu.VMEM((2, 4, SLOT, HD), BF16),
            pltpu.VMEM((2, SPAN, HD), BF16),
            pltpu.VMEM((2, SPAN + 4 * TXT, HD), BF16),
            pltpu.VMEM((4 * TXT, HD), BF16),
            pltpu.VMEM((states, HD), F32),
            pltpu.VMEM((states, HD), F32),
            pltpu.VMEM((states, HD), F32),
            pltpu.VMEM((2, 4, SLOT, HD), BF16),
            pltpu.VMEM((2, 4, 2, 8, HALF), F32),
            pltpu.VMEM((4 * TXT, 2 * HD), F32),
            pltpu.VMEM((2, 4, 2, HALF, HD), BF16),
            pltpu.VMEM((2, 4, 2, 8, HALF), F32),
            pltpu.VMEM((4, 2, TXT, 2 * HD), F32),
            DMA((2,)), DMA((8, 2)), DMA((8, 2)), DMA((2,)), DMA,
        ]
        + [DMA((2, 4, 2))] * 4 + [DMA((4,))] * 4 + [DMA((2, 4, 2))] * 4 + [DMA((4, 2))] * 2,
        compiler_params=pltpu.CompilerParams(collective_id=0, has_side_effects=True),
        name="mix",
    )(xv, xt, mv, mt, gv, gt, wv, wt)


def finish_kernel(
    heads, theads, mv, mt, wv_hbm, wt_hbm, video_out, text_out,
    pb, fb, nb, zb, zs, tp, trb, tfin, tall, wv, wt,
    wsem, fs, fr, ns, nr, zsem, zr, tss, trs, bs, br, xs, xr,
):
    me = Place()
    c = me.c
    half_cols = D // 2
    load_v = pltpu.make_async_copy(wv_hbm, wv, wsem.at[0])
    cols = pl.ds(pl.multiple_of(c * half_cols, half_cols), half_cols)
    load_t = pltpu.make_async_copy(wt_hbm.at[:, cols], wt, wsem.at[1])
    load_v.start()
    load_t.start()
    piece_y, piece_zh, half = me.piece()
    mine = me.y * 2 + me.zh
    home = me.zl // 2 == c

    def gatherer(k):
        return me.at(x=k, zl=2 * c + half, y=piece_y, zh=piece_zh)

    def giver(s):
        y, zh = s // 2, s % 2
        side = jnp.where(me.zh == zh, 0, 1)
        return me.at(x=lax.rem(me.y + 4 - y, 4), zl=2 * side + half, y=y, zh=zh)

    own_piece = jnp.logical_and(me.x == 0, jnp.logical_and(me.zl < 2, c == 0))
    column = [me.at(zl=lax.rem(me.zl + d, 4), c=r) for d in range(4) for r in (c, 1 - c)]
    across = [me.at(x=lax.rem(me.x + d, 4)) for d in range(1, 4)]
    up, down = me.group(1, 0), me.group(3, 0)
    arrived = greet(
        [up, down, me.group(0, 1)] + column[1:] + across,
        4 - jnp.where(own_piece, 1, 0),
    )
    barrier = pltpu.get_barrier_semaphore()

    @pl.when(home)
    def _():
        for s in range(8):
            @pl.when(jnp.logical_not(jnp.logical_and(own_piece, s == mine)))
            def _():
                pl.semaphore_signal(barrier, inc=1, device_id=giver(s), device_id_type=MESH)

    load_t.wait()
    part = jnp.dot(theads[...], wt[...], preferred_element_type=F32).astype(BF16)
    for k in range(4):
        tp[k] = part[:, k * (D // 8) : (k + 1) * (D // 8)]
    load_v.wait()

    def block(p):
        lhs = heads[p * 4 * CHUNK : (p + 1) * 4 * CHUNK, :]
        for q in range(4):
            span = slice(q * (D // 4), (q + 1) * (D // 4))
            found = jnp.dot(lhs, wv[:, span], preferred_element_type=F32).astype(BF16)
            pb[4 * p : 4 * p + 4, :, span] = found.reshape(4, CHUNK, D // 4)

    block(1)
    arrived()

    far_device = me.at(y=lax.rem(me.y + 3 + 2 * c, 4))
    near_slot = 3 - 2 * c
    plain_device = me.at(y=lax.rem(me.y + 1 + 2 * c, 4))
    plain_slot = 1 + 2 * c

    def part_of(h):
        return pl.ds(h * half_cols, half_cols)

    def far_copy(p, h):
        return remote(
            pb.at[4 * p + 2, :, part_of(h)], fb.at[p, :, part_of(h)],
            fs.at[p, h], fr.at[p, h], far_device,
        )

    def plain_copy(p, h):
        return remote(
            pb.at[4 * p + plain_slot, :, part_of(h)], nb.at[p, 0, :, part_of(h)],
            ns.at[p, 0, h], nr.at[p, 0, h], plain_device,
        )

    def sum_copy(p, h):
        return remote(
            pb.at[4 * p + near_slot, :, part_of(h)], nb.at[p, 1, :, part_of(h)],
            ns.at[p, 1, h], nr.at[p, 1, h], far_device,
        )

    def mirror_copy(h):
        return remote(
            zs.at[:, part_of(h)], zb.at[:, part_of(h)], zsem.at[h], zr.at[h], me.group(0, 1)
        )

    def depart(p):
        for h in range(2):
            far_copy(p, h).start()
            plain_copy(p, h).start()

    def relay(p, h):
        far_copy(p, h).wait_recv()
        at = part_of(h)
        total = pb[4 * p + near_slot, :, at].astype(F32) + fb[p, :, at].astype(F32)
        pb[4 * p + near_slot, :, at] = total.astype(BF16)
        sum_copy(p, h).start()

    def collect(p, h):
        plain_copy(p, h).wait_recv()
        sum_copy(p, h).wait_recv()
        at = part_of(h)
        return (
            pb[4 * p, :, at].astype(F32) + nb[p, 0, :, at].astype(F32) + nb[p, 1, :, at].astype(F32)
        )

    depart(1)
    text_parts = [
        remote(tp.at[k], trb.at[mine], tss.at[k], trs.at[mine], gatherer(k)) for k in range(4)
    ]
    own_part = pltpu.make_async_copy(tp.at[0], trb.at[mine], trs.at[mine])

    @pl.when(own_piece)
    def _():
        own_part.start()

    @pl.when(jnp.logical_not(own_piece))
    def _():
        text_parts[0].start()

    for text_part in text_parts[1:]:
        text_part.start()
    block(0)
    relay(1, 0)
    relay(1, 1)
    depart(0)
    for h in range(2):
        zs[:, part_of(h)] = collect(1, h).astype(BF16)
        mirror_copy(h).start()

    shares = [
        remote(tfin, tall.at[me.x, half, c], bs.at[i], br.at[half, c], device)
        for i, device in enumerate(column[1:])
    ]

    @pl.when(home)
    def _():
        total = jnp.zeros((TXT, D // 8), F32)
        for s in range(8):
            pltpu.make_async_copy(trb.at[s], trb.at[s], trs.at[s]).wait()
            total = total + trb[s].astype(F32)
        width = D // 8
        at = pl.ds(pl.multiple_of(c * half_cols + me.x * width, width), width)
        tfin[...] = (total * mt[2:3, at].astype(F32)).astype(BF16)
        for share in shares:
            share.start()
        tall[me.x, half, c] = tfin[...]

    relay(0, 0)
    relay(0, 1)
    for b in range(2):
        for r in range(2):
            @pl.when(jnp.logical_not(jnp.logical_and(home, jnp.logical_and(half == b, c == r))))
            def _():
                dst = tall.at[me.x, b, r]
                pltpu.make_async_copy(dst, dst, br.at[b, r]).wait()

    spreads = [
        remote(tall.at[me.x], tall.at[me.x], xs.at[d], xr.at[d], device)
        for d, device in enumerate(across)
    ]
    for copy in spreads:
        copy.start()
    for h in range(2):
        summed = collect(0, h)
        mirror_copy(h).wait_recv()
        at = part_of(h)
        summed = summed + zb[:, at].astype(F32)
        video_out[:, at] = (summed * mv[2:3, at].astype(F32)).astype(BF16)

    for copy in spreads:
        copy.wait_recv()
    for k in range(4):
        for b in range(2):
            for r in range(2):
                at = r * half_cols + k * (D // 8)
                text_out[b * TXT : (b + 1) * TXT, at : at + D // 8] = tall[k, b, r]
    for h in range(2):
        for p in (0, 1):
            far_copy(p, h).wait_send()
            plain_copy(p, h).wait_send()
            sum_copy(p, h).wait_send()
        mirror_copy(h).wait_send()

    @pl.when(jnp.logical_not(own_piece))
    def _():
        text_parts[0].wait_send()

    for copy in text_parts[1:] + spreads:
        copy.wait_send()

    @pl.when(home)
    def _():
        for share in shares:
            share.wait_send()


def finish(heads, theads, mv, mt, wv, wt):
    half_cols = D // 2
    return pl.pallas_call(
        finish_kernel,
        out_shape=(
            jax.ShapeDtypeStruct((CHUNK, D), BF16),
            jax.ShapeDtypeStruct((2 * TXT, D), BF16),
        ),
        in_specs=vmem(4) + hbm(2),
        out_specs=tuple(vmem(2)),
        scratch_shapes=[
            pltpu.VMEM((8, CHUNK, D), BF16),
            pltpu.VMEM((2, CHUNK, D), BF16),
            pltpu.VMEM((2, 2, CHUNK, D), BF16),
            pltpu.VMEM((CHUNK, D), BF16),
            pltpu.VMEM((CHUNK, D), BF16),
            pltpu.VMEM((4, TXT, D // 8), BF16),
            pltpu.VMEM((8, TXT, D // 8), BF16),
            pltpu.VMEM((TXT, D // 8), BF16),
            pltpu.VMEM((4, 2, 2, TXT, D // 8), BF16),
            pltpu.VMEM((2 * HD, D), BF16),
            pltpu.VMEM((2 * HD, half_cols), BF16),
            DMA((2,)), DMA((2, 2)), DMA((2, 2)), DMA((2, 2, 2)), DMA((2, 2, 2)), DMA((2,)), DMA((2,)),
            DMA((4,)), DMA((8,)), DMA((7,)), DMA((2, 2)), DMA((3,)), DMA((3,)),
        ],
        compiler_params=pltpu.CompilerParams(collective_id=1, has_side_effects=True),
        name="finish",
    )(heads, theads, mv, mt, wv, wt)


def local(
    video_tokens, text_tokens, video_modulation, text_modulation, video_projection,
    text_projection, video_output, text_output, video_gains, text_gains,
):
    heads, theads = mix(
        video_tokens, text_tokens, video_modulation, text_modulation, video_gains, text_gains,
        jnp.transpose(video_projection, (1, 0, 2)), jnp.transpose(text_projection, (1, 0, 2)),
    )
    return finish(heads, theads, video_modulation, text_modulation, video_output, text_output)


def solution(mesh):
    torus = Mesh(mesh.devices.reshape(4, 4, 2, 4, 2), AX)
    placed = (
        P(AX, None),
        P(ULY, None),
        P(),
        P(),
        P(None, None, ULY),
        P(None, None, ULY),
        P(ULY, None),
        P(ULY, None),
        P(),
        P(),
    )
    return jax.shard_map(
        local,
        mesh=torus,
        in_specs=placed,
        out_specs=(P(AX, None), P(ULY, None)),
        check_vma=False,
    )
```

```python
import math

import jax
import jax.numpy as jnp
from jax import lax
from jax.experimental import pallas as pl
from jax.experimental.pallas import tpu as pltpu
from jax.sharding import Mesh
from jax.sharding import PartitionSpec as P

D = 3072
HD = 128
EPS = 1e-06
MESH = pl.DeviceIdType.MESH
AX = ("x", "zl", "c", "y", "zh")
ULY = ("y", "zh")
CHUNK = 48
ROWS = 8 * CHUNK
TXT = 16
LOG2 = math.log2(math.e) / math.sqrt(HD)
F32 = jnp.float32
BF16 = jnp.bfloat16


class Place:
    def __init__(self):
        self.x, self.zl, self.c, self.y, self.zh = (lax.axis_index(a) for a in AX)

    def at(self, **moved):
        found = {"x": self.x, "zl": self.zl, "c": self.c, "y": self.y, "zh": self.zh}
        found.update(moved)
        return found

    def group(self, dy, dz):
        y = lax.rem(self.y + dy, 4)
        if dz:
            return self.at(y=y, zh=1 - self.zh, zl=3 - self.zl)
        return self.at(y=y)

    def piece(self):
        return lax.rem(self.y + self.x, 4), jnp.where(self.zl < 2, self.zh, 1 - self.zh), lax.rem(self.zl, 2)


GROUP = [(dy, dz) for dz in (0, 1) for dy in range(4) if (dy, dz) != (0, 0)]


def greet(devices, more=0):
    barrier = pltpu.get_barrier_semaphore()
    for device in devices:
        pl.semaphore_signal(barrier, inc=1, device_id=device, device_id_type=MESH)
    return lambda: pl.semaphore_wait(barrier, len(devices) + more)


def remote(src, dst, ssem, rsem, device):
    return pltpu.make_async_remote_copy(
        src_ref=src, dst_ref=dst, send_sem=ssem, recv_sem=rsem,
        device_id=device, device_id_type=MESH,
    )


def modulate(rows, factors):
    floats = rows.astype(F32)
    centre = floats - jnp.mean(floats, axis=-1, keepdims=True)
    spread = jnp.mean(centre * centre, axis=-1, keepdims=True)
    normed = centre / jnp.sqrt(spread + EPS)
    return (normed * (1.0 + factors[1:2].astype(F32)) + factors[0:1].astype(F32)).astype(BF16)


def head_norm(vectors, gain):
    inverse = lax.rsqrt(jnp.mean(vectors * vectors, axis=-1, keepdims=True) + EPS)
    return (vectors * inverse * gain).astype(BF16)


HALF = ROWS // 2
SLOT = 2 * HALF
SPAN = 4 * SLOT


def mix_kernel(
    xv, xt, mv, mt, gv, gt, wv_hbm, wt_hbm, heads, theads,
    rows, ttmp, trow, wv, wt, qkv, tqkv, qb, kva, kvb, tq, mb, lb, ab,
    ob, sb, tob, orecv, srecv, trecv,
    wsem, gs, gr, tgs, tgr,
    kvs, kvr, qs, qr, tks, tkr, tqs, tqr, os_, or_, ss, sr, ts, tr,
):
    me = Place()
    c = me.c
    other = 1 - c
    load_v = pltpu.make_async_copy(wv_hbm, wv, wsem.at[0])
    load_t = pltpu.make_async_copy(
        wt_hbm.at[:, :, pl.ds(pl.multiple_of(c * HD, HD), HD)], wt, wsem.at[1]
    )
    load_v.start()
    load_t.start()
    peers = [me.group(dy, dz) for dy, dz in GROUP] + [me.at(c=other)]
    for d in range(1, 4):
        for r in (c, other):
            peers.append(me.at(x=lax.rem(me.x + d, 4), c=r))
            peers.append(me.at(zl=lax.rem(me.zl + d, 4), c=r))
    arrived = greet(peers)
    rows[0] = modulate(xv[...], mv[...])
    low_chip = me.zl < 2
    stays = jnp.logical_and(low_chip, me.x == 0)

    @pl.when(low_chip)
    def _():
        for b in range(2):
            ttmp[b] = modulate(xt[b * TXT : (b + 1) * TXT, :], mt[...])

    @pl.when(stays)
    def _():
        trow[...] = ttmp[me.zl]

    arrived()


    def copy_rows(src, dst, device):
        return [
            remote(
                rows.at[src, :, pl.ds(h * (D // 2), D // 2)], rows.at[dst, :, pl.ds(h * (D // 2), D // 2)],
                gs.at[dst, h], gr.at[dst, h], device,
            )
            for h in range(2)
        ]

    up, down = me.group(1, 0), me.group(3, 0)
    far_src = 3 - 2 * c
    far_device = me.at(y=lax.rem(me.y + 1 + 2 * c, 4))
    mirror = copy_rows(0, 4, me.group(0, 1))
    moves = [
        (copy_rows(b, b + 1, down), copy_rows(b, b + 3, up), copy_rows(b + far_src, b + 2, far_device))
        for b in (0, 4)
    ]

    def spread(p, h):
        low, high, _ = moves[p]
        high[h].start()
        low[h].start()

    def onward(p, h):
        low, high, far = moves[p]

        @pl.when(c == 0)
        def _():
            high[h].wait_recv()

        @pl.when(c == 1)
        def _():
            low[h].wait_recv()

        far[h].start()

    def gathered(p):
        low, high, far = moves[p]

        @pl.when(c == 0)
        def _():
            for copy in low:
                copy.wait_recv()

        @pl.when(c == 1)
        def _():
            for copy in high:
                copy.wait_recv()

        for copy in far:
            copy.wait_recv()

    text_y = lax.rem(me.y + 4 - me.x, 4)
    text_near = remote(ttmp.at[lax.rem(me.zl, 2)], trow, tgs.at[0], tgr, me.at(y=text_y))
    text_over = remote(
        ttmp.at[1 - lax.rem(me.zl, 2)], trow, tgs.at[1], tgr,
        me.at(y=text_y, zh=1 - me.zh, zl=3 - me.zl),
    )

    def block(p):
        lhs = rows[4 * p : 4 * p + 4].reshape(HALF, D)
        for j in range(3):
            total = jnp.dot(lhs, wv[j], preferred_element_type=F32)
            for h in range(2):
                part = total[:, h * HD : (h + 1) * HD]
                part = head_norm(part, gv[j : j + 1]) if j < 2 else part.astype(BF16)
                qkv[h, p, j] = part


    sends = []

    def send(copy):
        copy.start()
        sends.append(copy)

    def kv_rows(p, slot, core):
        at = pl.ds(pl.multiple_of(slot * SLOT + core * HALF, HALF), HALF)
        return (kvb if p else kva).at[:, at, :]

    def q_rows(p, slot, core):
        return qb.at[p, slot, pl.ds(pl.multiple_of(core * HALF, HALF), HALF), :]

    def kv_text(slot):
        return kvb.at[:, pl.ds(SPAN + TXT * slot, TXT), :]

    def q_text(slot):
        return tq.at[pl.ds(TXT * slot, TXT), :]

    def along(axis, d, r):
        return me.at(**{axis: lax.rem(getattr(me, axis) + d, 4), "c": r})

    def exchange(p):
        pltpu.make_async_copy(qkv.at[c, p, 0], q_rows(p, 0, c), qr.at[p, 0, 0]).start()
        pltpu.make_async_copy(
            qkv.at[c, p, pl.ds(1, 2)], kv_rows(p, 0, c), kvr.at[p, 0, 0]
        ).start()
        for d in (0, 3, 1, 2):
            slot = (4 - d) % 4
            for i, r in enumerate((c, other)):
                if d or i:
                    send(remote(
                        qkv.at[r, p, 0], q_rows(p, slot, c),
                        qs.at[p, slot, i], qr.at[p, slot, i], along("zl", d, r),
                    ))
            for i, r in enumerate((c, other)):
                if d or i:
                    send(remote(
                        qkv.at[r, p, pl.ds(1, 2)], kv_rows(p, slot, c),
                        kvs.at[p, slot, i], kvr.at[p, slot, i], along("x", d, r),
                    ))

    def exchange_text():
        pltpu.make_async_copy(tqkv.at[0], q_text(0), tqr.at[0]).start()
        pltpu.make_async_copy(tqkv.at[pl.ds(1, 2)], kv_text(0), tkr.at[0]).start()
        for d in (3, 1, 2):
            slot = (4 - d) % 4
            send(remote(tqkv.at[0], q_text(slot), tqs.at[slot], tqr.at[slot], along("zl", d, c)))
            send(remote(
                tqkv.at[pl.ds(1, 2)], kv_text(slot), tks.at[slot], tkr.at[slot], along("x", d, c)
            ))

    def landed(dst, sem):
        pltpu.make_async_copy(dst, dst, sem).wait()

    def await_kv(p):
        for slot in (0, 1, 3, 2):
            for i in range(2):
                landed(kv_rows(p, slot, i), kvr.at[p, slot, i])

    def await_q(p, slot):
        for i in range(2):
            landed(q_rows(p, slot, i), qr.at[p, slot, i])

    def scored(queries, keys):
        return lax.dot_general(
            queries, keys, (((1,), (1,)), ((), ())), preferred_element_type=F32
        )

    def lanes(weights):
        width = weights.shape[1]
        if width % HD:
            extra = weights[:, width - width % HD :]
            pad = jnp.zeros((extra.shape[0], HD - width % HD), F32)
            total = jnp.concatenate([extra, pad], axis=1)
        else:
            total = jnp.zeros((weights.shape[0], HD), F32)
        for k in range(width // HD):
            total = total + weights[:, k * HD : (k + 1) * HD]
        return total

    def open_step(queries, at):
        scores = scored(queries, kva[0])
        now = jnp.max(scores, axis=-1, keepdims=True)
        weights = jnp.exp2((scores - now) * LOG2)
        mb[at, :] = jnp.broadcast_to(now, (queries.shape[0], HD))
        lb[at, :] = lanes(weights)
        ab[at, :] = jnp.dot(weights.astype(BF16), kva[1], preferred_element_type=F32)

    def last_step(queries, at):
        scores = scored(queries, kvb[0])
        before = mb[at, :]
        now = jnp.maximum(before[:, :1], jnp.max(scores, axis=-1, keepdims=True))
        weights = jnp.exp2((scores - now) * LOG2)
        shrink = jnp.exp2((before - now) * LOG2)
        totals = jnp.sum(lb[at, :] * shrink + lanes(weights), axis=-1, keepdims=True)
        sums = ab[at, :] * shrink + jnp.dot(
            weights.astype(BF16), kvb[1], preferred_element_type=F32
        )
        level = jnp.broadcast_to(now * LOG2 + jnp.log2(totals), sums.shape)
        return sums / totals, level

    tail = pl.ds(2 * SPAN, 4 * TXT)

    def state_rows(p, slot):
        return pl.ds(pl.multiple_of((p * 4 + slot) * SLOT, SLOT), SLOT)

    def open_phase(p):
        def pair(i, _):
            slots = (3 * i, 1 + i)
            for slot in slots:
                await_q(p, slot)
            for slot in slots:
                open_step(qb[p, slot], state_rows(p, slot))
            return 0

        lax.fori_loop(0, 2, pair, 0)

    def out_copies(p, j, slot, i, r):
        device = along("zl", j, r)
        return (
            remote(
                ob.at[p, j, pl.ds(pl.multiple_of(r * HALF, HALF), HALF), :], orecv.at[p, slot, c],
                os_.at[p, slot, i], or_.at[p, slot, i], device,
            ),
            remote(
                sb.at[p, j, r], srecv.at[p, slot, c], ss.at[p, slot, i], sr.at[p, slot, i], device
            ),
        )

    def last_phase(p):
        def pair(n, _):
            slots = (2 - 2 * n, 3 - 2 * n)
            for slot in slots:
                mixed, level = last_step(qb[p, slot], state_rows(p, slot))
                ob[p, slot] = mixed.astype(BF16)
                for r in range(2):
                    part = level[r * HALF : (r + 1) * HALF]
                    sb[p, slot, r] = jnp.transpose(part)[:8, :]

            @pl.when(n == 0)
            def _():
                for j in (2, 3):
                    for i, r in enumerate((c, other)):
                        for copy in out_copies(p, j, 4 - j, i, r):
                            copy.start()

            @pl.when(n == 1)
            def _():
                for i, r in enumerate((c, other)):
                    for copy in out_copies(p, 1, 3, i, r):
                        copy.start()
                for copy in out_copies(p, 0, 0, 1, other):
                    copy.start()
                at = pl.ds(pl.multiple_of(c * HALF, HALF), HALF)
                pltpu.make_async_copy(
                    ob.at[p, 0, at, :], orecv.at[p, 0, c], or_.at[p, 0, 0]
                ).start()
                pltpu.make_async_copy(sb.at[p, 0, c], srecv.at[p, 0, c], sr.at[p, 0, 0]).start()

            return 0

        lax.fori_loop(0, 2, pair, 0)

    def merge(p):
        for slot in range(4):
            for i, r in enumerate((c, other)):
                landed(orecv.at[p, slot, r], or_.at[p, slot, i])
                landed(srecv.at[p, slot, r], sr.at[p, slot, i])
        for h in range(2):
            found = [srecv[p, slot, h] for slot in range(4)]
            top = jnp.maximum(jnp.maximum(found[0], found[1]), jnp.maximum(found[2], found[3]))
            weight = [jnp.exp2(part - top) for part in found]
            share = 1.0 / sum(weight)
            mixed = jnp.zeros((HALF, HD), F32)
            for slot in range(4):
                row = (weight[slot] * share)[:1]
                column = jnp.transpose(jnp.broadcast_to(row, (HD, HALF)))
                mixed = mixed + column * orecv[p, slot, h].astype(F32)
            heads[p * HALF : (p + 1) * HALF, h * HD : (h + 1) * HD] = mixed.astype(BF16)

    def send_text():
        mixed, level = last_step(tq[...], tail)
        tob[:, :HD] = mixed
        tob[:, HD:] = level
        for j in range(4):
            slot = (4 - j) % 4
            for i, r in enumerate((c, other)):
                src, dst = tob.at[pl.ds(TXT * j, TXT), :], trecv.at[slot, c]
                if j == 0 and i == 0:
                    pltpu.make_async_copy(src, dst, tr.at[0, 0]).start()
                else:
                    send(remote(src, dst, ts.at[slot, i], tr.at[slot, i], along("zl", j, r)))

    def merge_text():
        for slot in range(4):
            for i, r in enumerate((c, other)):
                landed(trecv.at[slot, r], tr.at[slot, i])
        for h in range(2):
            found = [trecv[slot, h] for slot in range(4)]
            top = found[0][:, HD:]
            for part in found[1:]:
                top = jnp.maximum(top, part[:, HD:])
            weight = [jnp.exp2(part[:, HD:] - top) for part in found]
            mixed = sum(w * part[:, :HD] for w, part in zip(weight, found)) / sum(weight)
            theads[:, h * HD : (h + 1) * HD] = mixed.astype(BF16)

    mirror[0].start()
    spread(0, 0)
    mirror[1].start()
    spread(0, 1)

    @pl.when(low_chip)
    def _():
        text_over.start()

    @pl.when(jnp.logical_and(low_chip, me.x > 0))
    def _():
        text_near.start()

    onward(0, 0)
    onward(0, 1)
    for h in range(2):
        mirror[h].wait_recv()
        spread(1, h)
    load_v.wait()
    gathered(0)
    block(0)
    exchange(0)
    onward(1, 0)
    onward(1, 1)

    @pl.when(jnp.logical_not(stays))
    def _():
        text_near.wait_recv()

    load_t.wait()
    for j in range(3):
        part = jnp.dot(trow[...], wt[j], preferred_element_type=F32)
        tqkv[j] = head_norm(part, gt[j : j + 1]) if j < 2 else part.astype(BF16)
    exchange_text()
    gathered(1)
    block(1)
    exchange(1)
    await_kv(0)
    open_phase(0)
    for j in range(4):
        landed(q_text(j), tqr.at[j])
    open_step(tq[...], tail)
    open_phase(1)
    await_kv(1)
    for j in range(4):
        landed(kv_text(j), tkr.at[j])
    send_text()
    last_phase(1)
    last_phase(0)
    merge_text()
    merge(1)
    merge(0)

    for pair in [mirror] + [found for move in moves for found in move]:
        for copy in pair:
            copy.wait_send()

    @pl.when(low_chip)
    def _():
        text_over.wait_send()

    @pl.when(jnp.logical_and(low_chip, me.x > 0))
    def _():
        text_near.wait_send()

    for copy in sends:
        copy.wait_send()
    for p in range(2):
        for slot in range(4):
            for i, r in enumerate((c, other)):
                if (slot, i) != (0, 0):
                    for copy in out_copies(p, (4 - slot) % 4, slot, i, r):
                        copy.wait_send()


def vmem(n):
    return [pl.BlockSpec(memory_space=pltpu.VMEM)] * n


def hbm(n):
    return [pl.BlockSpec(memory_space=pl.ANY)] * n


DMA = pltpu.SemaphoreType.DMA


def mix(xv, xt, mv, mt, gv, gt, wv, wt):
    states = 2 * SPAN + 4 * TXT
    return pl.pallas_call(
        mix_kernel,
        out_shape=(
            jax.ShapeDtypeStruct((ROWS, 2 * HD), BF16),
            jax.ShapeDtypeStruct((TXT, 2 * HD), BF16),
        ),
        in_specs=vmem(6) + hbm(2),
        out_specs=tuple(vmem(2)),
        scratch_shapes=[
            pltpu.VMEM((8, CHUNK, D), BF16),
            pltpu.VMEM((2, TXT, D), BF16),
            pltpu.VMEM((TXT, D), BF16),
            pltpu.VMEM((3, D, 2 * HD), BF16),
            pltpu.VMEM((3, D, HD), BF16),
            pltpu.VMEM((2, 2, 3, HALF, HD), BF16),
            pltpu.VMEM((3, TXT, HD), BF16),
            pltpu.VMEM((2, 4, SLOT, HD), BF16),
            pltpu.VMEM((2, SPAN, HD), BF16),
            pltpu.VMEM((2, SPAN + 4 * TXT, HD), BF16),
            pltpu.VMEM((4 * TXT, HD), BF16),
            pltpu.VMEM((states, HD), F32),
            pltpu.VMEM((states, HD), F32),
            pltpu.VMEM((states, HD), F32),
            pltpu.VMEM((2, 4, SLOT, HD), BF16),
            pltpu.VMEM((2, 4, 2, 8, HALF), F32),
            pltpu.VMEM((4 * TXT, 2 * HD), F32),
            pltpu.VMEM((2, 4, 2, HALF, HD), BF16),
            pltpu.VMEM((2, 4, 2, 8, HALF), F32),
            pltpu.VMEM((4, 2, TXT, 2 * HD), F32),
            DMA((2,)), DMA((8, 2)), DMA((8, 2)), DMA((2,)), DMA,
        ]
        + [DMA((2, 4, 2))] * 4 + [DMA((4,))] * 4 + [DMA((2, 4, 2))] * 4 + [DMA((4, 2))] * 2,
        compiler_params=pltpu.CompilerParams(collective_id=0, has_side_effects=True),
        name="mix",
    )(xv, xt, mv, mt, gv, gt, wv, wt)


def finish_kernel(
    heads, theads, mv, mt, wv_hbm, wt_hbm, video_out, text_out,
    pb, fb, nb, zb, zs, tp, trb, tfin, tall, wv, wt,
    wsem, fs, fr, ns, nr, zsem, zr, tss, trs, bs, br, xs, xr,
):
    me = Place()
    c = me.c
    half_cols = D // 2
    load_v = pltpu.make_async_copy(wv_hbm, wv, wsem.at[0])
    cols = pl.ds(pl.multiple_of(c * half_cols, half_cols), half_cols)
    load_t = pltpu.make_async_copy(wt_hbm.at[:, cols], wt, wsem.at[1])
    load_v.start()
    load_t.start()
    piece_y, piece_zh, half = me.piece()
    mine = me.y * 2 + me.zh
    home = me.zl // 2 == c

    def gatherer(k):
        return me.at(x=k, zl=2 * c + half, y=piece_y, zh=piece_zh)

    def giver(s):
        y, zh = s // 2, s % 2
        side = jnp.where(me.zh == zh, 0, 1)
        return me.at(x=lax.rem(me.y + 4 - y, 4), zl=2 * side + half, y=y, zh=zh)

    own_piece = jnp.logical_and(me.x == 0, jnp.logical_and(me.zl < 2, c == 0))
    column = [me.at(zl=lax.rem(me.zl + d, 4), c=r) for d in range(4) for r in (c, 1 - c)]
    across = [me.at(x=lax.rem(me.x + d, 4)) for d in range(1, 4)]
    up, down = me.group(1, 0), me.group(3, 0)
    arrived = greet(
        [up, down, me.group(0, 1)] + column[1:] + across,
        4 - jnp.where(own_piece, 1, 0),
    )
    barrier = pltpu.get_barrier_semaphore()

    @pl.when(home)
    def _():
        for s in range(8):
            @pl.when(jnp.logical_not(jnp.logical_and(own_piece, s == mine)))
            def _():
                pl.semaphore_signal(barrier, inc=1, device_id=giver(s), device_id_type=MESH)

    load_t.wait()
    part = jnp.dot(theads[...], wt[...], preferred_element_type=F32).astype(BF16)
    for k in range(4):
        tp[k] = part[:, k * (D // 8) : (k + 1) * (D // 8)]
    load_v.wait()

    def block(p):
        lhs = heads[p * 4 * CHUNK : (p + 1) * 4 * CHUNK, :]
        for q in range(4):
            span = slice(q * (D // 4), (q + 1) * (D // 4))
            found = jnp.dot(lhs, wv[:, span], preferred_element_type=F32).astype(BF16)
            pb[4 * p : 4 * p + 4, :, span] = found.reshape(4, CHUNK, D // 4)

    block(1)
    arrived()

    far_device = me.at(y=lax.rem(me.y + 3 + 2 * c, 4))
    near_slot = 3 - 2 * c
    plain_device = me.at(y=lax.rem(me.y + 1 + 2 * c, 4))
    plain_slot = 1 + 2 * c

    def part_of(h):
        return pl.ds(h * half_cols, half_cols)

    def far_copy(p, h):
        return remote(
            pb.at[4 * p + 2, :, part_of(h)], fb.at[p, :, part_of(h)],
            fs.at[p, h], fr.at[p, h], far_device,
        )

    def plain_copy(p, h):
        return remote(
            pb.at[4 * p + plain_slot, :, part_of(h)], nb.at[p, 0, :, part_of(h)],
            ns.at[p, 0, h], nr.at[p, 0, h], plain_device,
        )

    def sum_copy(p, h):
        return remote(
            pb.at[4 * p + near_slot, :, part_of(h)], nb.at[p, 1, :, part_of(h)],
            ns.at[p, 1, h], nr.at[p, 1, h], far_device,
        )

    def mirror_copy(h):
        return remote(
            zs.at[:, part_of(h)], zb.at[:, part_of(h)], zsem.at[h], zr.at[h], me.group(0, 1)
        )

    def depart(p):
        for h in range(2):
            far_copy(p, h).start()
            plain_copy(p, h).start()

    def relay(p, h):
        far_copy(p, h).wait_recv()
        at = part_of(h)
        total = pb[4 * p + near_slot, :, at].astype(F32) + fb[p, :, at].astype(F32)
        pb[4 * p + near_slot, :, at] = total.astype(BF16)
        sum_copy(p, h).start()

    def collect(p, h):
        plain_copy(p, h).wait_recv()
        sum_copy(p, h).wait_recv()
        at = part_of(h)
        return (
            pb[4 * p, :, at].astype(F32) + nb[p, 0, :, at].astype(F32) + nb[p, 1, :, at].astype(F32)
        )

    depart(1)
    text_parts = [
        remote(tp.at[k], trb.at[mine], tss.at[k], trs.at[mine], gatherer(k)) for k in range(4)
    ]
    own_part = pltpu.make_async_copy(tp.at[0], trb.at[mine], trs.at[mine])

    @pl.when(own_piece)
    def _():
        own_part.start()

    @pl.when(jnp.logical_not(own_piece))
    def _():
        text_parts[0].start()

    for text_part in text_parts[1:]:
        text_part.start()
    block(0)
    relay(1, 0)
    relay(1, 1)
    depart(0)
    for h in range(2):
        zs[:, part_of(h)] = collect(1, h).astype(BF16)
        mirror_copy(h).start()

    shares = [
        remote(tfin, tall.at[me.x, half, c], bs.at[i], br.at[half, c], device)
        for i, device in enumerate(column[1:])
    ]

    @pl.when(home)
    def _():
        total = jnp.zeros((TXT, D // 8), F32)
        for s in range(8):
            pltpu.make_async_copy(trb.at[s], trb.at[s], trs.at[s]).wait()
            total = total + trb[s].astype(F32)
        width = D // 8
        at = pl.ds(pl.multiple_of(c * half_cols + me.x * width, width), width)
        tfin[...] = (total * mt[2:3, at].astype(F32)).astype(BF16)
        for share in shares:
            share.start()
        tall[me.x, half, c] = tfin[...]

    relay(0, 0)
    relay(0, 1)
    for b in range(2):
        for r in range(2):
            @pl.when(jnp.logical_not(jnp.logical_and(home, jnp.logical_and(half == b, c == r))))
            def _():
                dst = tall.at[me.x, b, r]
                pltpu.make_async_copy(dst, dst, br.at[b, r]).wait()

    spreads = [
        remote(tall.at[me.x], tall.at[me.x], xs.at[d], xr.at[d], device)
        for d, device in enumerate(across)
    ]
    for copy in spreads:
        copy.start()
    for h in range(2):
        summed = collect(0, h)
        mirror_copy(h).wait_recv()
        at = part_of(h)
        summed = summed + zb[:, at].astype(F32)
        video_out[:, at] = (summed * mv[2:3, at].astype(F32)).astype(BF16)

    for copy in spreads:
        copy.wait_recv()
    for k in range(4):
        for b in range(2):
            for r in range(2):
                at = r * half_cols + k * (D // 8)
                text_out[b * TXT : (b + 1) * TXT, at : at + D // 8] = tall[k, b, r]
    for h in range(2):
        for p in (0, 1):
            far_copy(p, h).wait_send()
            plain_copy(p, h).wait_send()
            sum_copy(p, h).wait_send()
        mirror_copy(h).wait_send()

    @pl.when(jnp.logical_not(own_piece))
    def _():
        text_parts[0].wait_send()

    for copy in text_parts[1:] + spreads:
        copy.wait_send()

    @pl.when(home)
    def _():
        for share in shares:
            share.wait_send()


def finish(heads, theads, mv, mt, wv, wt):
    half_cols = D // 2
    return pl.pallas_call(
        finish_kernel,
        out_shape=(
            jax.ShapeDtypeStruct((CHUNK, D), BF16),
            jax.ShapeDtypeStruct((2 * TXT, D), BF16),
        ),
        in_specs=vmem(4) + hbm(2),
        out_specs=tuple(vmem(2)),
        scratch_shapes=[
            pltpu.VMEM((8, CHUNK, D), BF16),
            pltpu.VMEM((2, CHUNK, D), BF16),
            pltpu.VMEM((2, 2, CHUNK, D), BF16),
            pltpu.VMEM((CHUNK, D), BF16),
            pltpu.VMEM((CHUNK, D), BF16),
            pltpu.VMEM((4, TXT, D // 8), BF16),
            pltpu.VMEM((8, TXT, D // 8), BF16),
            pltpu.VMEM((TXT, D // 8), BF16),
            pltpu.VMEM((4, 2, 2, TXT, D // 8), BF16),
            pltpu.VMEM((2 * HD, D), BF16),
            pltpu.VMEM((2 * HD, half_cols), BF16),
            DMA((2,)), DMA((2, 2)), DMA((2, 2)), DMA((2, 2, 2)), DMA((2, 2, 2)), DMA((2,)), DMA((2,)),
            DMA((4,)), DMA((8,)), DMA((7,)), DMA((2, 2)), DMA((3,)), DMA((3,)),
        ],
        compiler_params=pltpu.CompilerParams(collective_id=1, has_side_effects=True),
        name="finish",
    )(heads, theads, mv, mt, wv, wt)


def settle_kernel(video, text, video_out, text_out):
    video_out[...] = video[...]
    text_out[...] = text[...]


def settle(video, text):
    return pl.pallas_call(
        settle_kernel,
        out_shape=tuple(jax.ShapeDtypeStruct(a.shape, a.dtype) for a in (video, text)),
        in_specs=vmem(2),
        out_specs=tuple(vmem(2)),
        name="settle",
    )(video, text)


def local(
    video_tokens, text_tokens, video_modulation, text_modulation, video_projection,
    text_projection, video_output, text_output, video_gains, text_gains,
):
    heads, theads = mix(
        video_tokens, text_tokens, video_modulation, text_modulation, video_gains, text_gains,
        jnp.transpose(video_projection, (1, 0, 2)), jnp.transpose(text_projection, (1, 0, 2)),
    )
    return settle(
        *finish(heads, theads, video_modulation, text_modulation, video_output, text_output)
    )


def solution(mesh):
    torus = Mesh(mesh.devices.reshape(4, 4, 2, 4, 2), AX)
    placed = (
        P(AX, None),
        P(ULY, None),
        P(),
        P(),
        P(None, None, ULY),
        P(None, None, ULY),
        P(ULY, None),
        P(ULY, None),
        P(),
        P(),
    )
    return jax.shard_map(
        local,
        mesh=torus,
        in_specs=placed,
        out_specs=(P(AX, None), P(ULY, None)),
        check_vma=False,
    )
```

```python
import math

import jax
import jax.numpy as jnp
from jax import lax
from jax.experimental import pallas as pl
from jax.experimental.pallas import tpu as pltpu
from jax.sharding import Mesh
from jax.sharding import PartitionSpec as P

D = 3072
HD = 128
EPS = 1e-06
MESH = pl.DeviceIdType.MESH
AX = ("x", "zl", "c", "y", "zh")
ULY = ("y", "zh")
CHUNK = 48
ROWS = 8 * CHUNK
TXT = 16
LOG2 = math.log2(math.e) / math.sqrt(HD)
F32 = jnp.float32
BF16 = jnp.bfloat16


class Place:
    def __init__(self):
        self.x, self.zl, self.c, self.y, self.zh = (lax.axis_index(a) for a in AX)

    def at(self, **moved):
        found = {"x": self.x, "zl": self.zl, "c": self.c, "y": self.y, "zh": self.zh}
        found.update(moved)
        return found

    def group(self, dy, dz):
        y = lax.rem(self.y + dy, 4)
        if dz:
            return self.at(y=y, zh=1 - self.zh, zl=3 - self.zl)
        return self.at(y=y)

    def piece(self):
        return lax.rem(self.y + self.x, 4), jnp.where(self.zl < 2, self.zh, 1 - self.zh), lax.rem(self.zl, 2)


GROUP = [(dy, dz) for dz in (0, 1) for dy in range(4) if (dy, dz) != (0, 0)]


def greet(devices, more=0):
    barrier = pltpu.get_barrier_semaphore()
    for device in devices:
        pl.semaphore_signal(barrier, inc=1, device_id=device, device_id_type=MESH)
    return lambda: pl.semaphore_wait(barrier, len(devices) + more)


def remote(src, dst, ssem, rsem, device):
    return pltpu.make_async_remote_copy(
        src_ref=src, dst_ref=dst, send_sem=ssem, recv_sem=rsem,
        device_id=device, device_id_type=MESH,
    )


def modulate(rows, factors):
    floats = rows.astype(F32)
    centre = floats - jnp.mean(floats, axis=-1, keepdims=True)
    spread = jnp.mean(centre * centre, axis=-1, keepdims=True)
    normed = centre / jnp.sqrt(spread + EPS)
    return (normed * (1.0 + factors[1:2].astype(F32)) + factors[0:1].astype(F32)).astype(BF16)


def head_norm(vectors, gain):
    inverse = lax.rsqrt(jnp.mean(vectors * vectors, axis=-1, keepdims=True) + EPS)
    return (vectors * inverse * gain).astype(BF16)


HALF = ROWS // 2
SLOT = 2 * HALF
SPAN = 4 * SLOT


def mix_kernel(
    xv, xt, mv, mt, gv, gt, wv_hbm, wt_hbm, heads, theads,
    rows, ttmp, trow, wv, wt, qkv, tqkv, qb, kva, kvb, tq, mb, lb, ab,
    ob, sb, tob, orecv, srecv, trecv,
    wsem, gs, gr, tgs, tgr,
    kvs, kvr, qs, qr, tks, tkr, tqs, tqr, os_, or_, ss, sr, ts, tr,
):
    me = Place()
    c = me.c
    other = 1 - c
    load_v = pltpu.make_async_copy(wv_hbm, wv, wsem.at[0])
    load_t = pltpu.make_async_copy(
        wt_hbm.at[:, :, pl.ds(pl.multiple_of(c * HD, HD), HD)], wt, wsem.at[1]
    )
    load_v.start()
    load_t.start()
    peers = [me.group(dy, dz) for dy, dz in GROUP] + [me.at(c=other)]
    for d in range(1, 4):
        for r in (c, other):
            peers.append(me.at(x=lax.rem(me.x + d, 4), c=r))
            peers.append(me.at(zl=lax.rem(me.zl + d, 4), c=r))
    arrived = greet(peers)
    rows[0] = modulate(xv[...], mv[...])
    low_chip = me.zl < 2
    stays = jnp.logical_and(low_chip, me.x == 0)

    @pl.when(low_chip)
    def _():
        for b in range(2):
            ttmp[b] = modulate(xt[b * TXT : (b + 1) * TXT, :], mt[...])

    @pl.when(stays)
    def _():
        trow[...] = ttmp[me.zl]

    arrived()


    def copy_rows(src, dst, device):
        return [
            remote(
                rows.at[src, :, pl.ds(h * (D // 2), D // 2)], rows.at[dst, :, pl.ds(h * (D // 2), D // 2)],
                gs.at[dst, h], gr.at[dst, h], device,
            )
            for h in range(2)
        ]

    up, down = me.group(1, 0), me.group(3, 0)
    far_src = 3 - 2 * c
    far_device = me.at(y=lax.rem(me.y + 1 + 2 * c, 4))
    mirror = copy_rows(0, 4, me.group(0, 1))
    moves = [
        (copy_rows(b, b + 1, down), copy_rows(b, b + 3, up), copy_rows(b + far_src, b + 2, far_device))
        for b in (0, 4)
    ]

    def spread(p, h):
        low, high, _ = moves[p]
        high[h].start()
        low[h].start()

    def onward(p, h):
        low, high, far = moves[p]

        @pl.when(c == 0)
        def _():
            high[h].wait_recv()

        @pl.when(c == 1)
        def _():
            low[h].wait_recv()

        far[h].start()

    def gathered(p):
        low, high, far = moves[p]

        @pl.when(c == 0)
        def _():
            for copy in low:
                copy.wait_recv()

        @pl.when(c == 1)
        def _():
            for copy in high:
                copy.wait_recv()

        for copy in far:
            copy.wait_recv()

    text_y = lax.rem(me.y + 4 - me.x, 4)
    text_near = remote(ttmp.at[lax.rem(me.zl, 2)], trow, tgs.at[0], tgr, me.at(y=text_y))
    text_over = remote(
        ttmp.at[1 - lax.rem(me.zl, 2)], trow, tgs.at[1], tgr,
        me.at(y=text_y, zh=1 - me.zh, zl=3 - me.zl),
    )

    def block(p):
        lhs = rows[4 * p : 4 * p + 4].reshape(HALF, D)
        for j in range(3):
            total = jnp.dot(lhs, wv[j], preferred_element_type=F32)
            for h in range(2):
                part = total[:, h * HD : (h + 1) * HD]
                part = head_norm(part, gv[j : j + 1]) if j < 2 else part.astype(BF16)
                qkv[h, p, j] = part


    sends = []

    def send(copy):
        copy.start()
        sends.append(copy)

    def kv_rows(p, slot, core):
        at = pl.ds(pl.multiple_of(slot * SLOT + core * HALF, HALF), HALF)
        return (kvb if p else kva).at[:, at, :]

    def q_rows(p, slot, core):
        return qb.at[p, slot, pl.ds(pl.multiple_of(core * HALF, HALF), HALF), :]

    def kv_text(slot):
        return kvb.at[:, pl.ds(SPAN + TXT * slot, TXT), :]

    def q_text(slot):
        return tq.at[pl.ds(TXT * slot, TXT), :]

    def along(axis, d, r):
        return me.at(**{axis: lax.rem(getattr(me, axis) + d, 4), "c": r})

    def exchange(p):
        pltpu.make_async_copy(qkv.at[c, p, 0], q_rows(p, 0, c), qr.at[p, 0, 0]).start()
        pltpu.make_async_copy(
            qkv.at[c, p, pl.ds(1, 2)], kv_rows(p, 0, c), kvr.at[p, 0, 0]
        ).start()
        for d in (0, 3, 1, 2):
            slot = (4 - d) % 4
            for i, r in enumerate((c, other)):
                if d or i:
                    send(remote(
                        qkv.at[r, p, 0], q_rows(p, slot, c),
                        qs.at[p, slot, i], qr.at[p, slot, i], along("zl", d, r),
                    ))
            for i, r in enumerate((c, other)):
                if d or i:
                    send(remote(
                        qkv.at[r, p, pl.ds(1, 2)], kv_rows(p, slot, c),
                        kvs.at[p, slot, i], kvr.at[p, slot, i], along("x", d, r),
                    ))

    def exchange_text():
        pltpu.make_async_copy(tqkv.at[0], q_text(0), tqr.at[0]).start()
        pltpu.make_async_copy(tqkv.at[pl.ds(1, 2)], kv_text(0), tkr.at[0]).start()
        for d in (3, 1, 2):
            slot = (4 - d) % 4
            send(remote(tqkv.at[0], q_text(slot), tqs.at[slot], tqr.at[slot], along("zl", d, c)))
            send(remote(
                tqkv.at[pl.ds(1, 2)], kv_text(slot), tks.at[slot], tkr.at[slot], along("x", d, c)
            ))

    def landed(dst, sem):
        pltpu.make_async_copy(dst, dst, sem).wait()

    def await_kv(p):
        for slot in (0, 1, 3, 2):
            for i in range(2):
                landed(kv_rows(p, slot, i), kvr.at[p, slot, i])

    def await_q(p, slot):
        for i in range(2):
            landed(q_rows(p, slot, i), qr.at[p, slot, i])

    def scored(queries, keys):
        return lax.dot_general(
            queries, keys, (((1,), (1,)), ((), ())), preferred_element_type=F32
        )

    def lanes(weights):
        width = weights.shape[1]
        if width % HD:
            extra = weights[:, width - width % HD :]
            pad = jnp.zeros((extra.shape[0], HD - width % HD), F32)
            total = jnp.concatenate([extra, pad], axis=1)
        else:
            total = jnp.zeros((weights.shape[0], HD), F32)
        for k in range(width // HD):
            total = total + weights[:, k * HD : (k + 1) * HD]
        return total

    def open_step(queries, at):
        scores = scored(queries, kva[0])
        now = jnp.max(scores, axis=-1, keepdims=True)
        weights = jnp.exp2((scores - now) * LOG2)
        mb[at, :] = jnp.broadcast_to(now, (queries.shape[0], HD))
        lb[at, :] = lanes(weights)
        ab[at, :] = jnp.dot(weights.astype(BF16), kva[1], preferred_element_type=F32)

    def last_step(queries, at):
        scores = scored(queries, kvb[0])
        before = mb[at, :]
        now = jnp.maximum(before[:, :1], jnp.max(scores, axis=-1, keepdims=True))
        weights = jnp.exp2((scores - now) * LOG2)
        shrink = jnp.exp2((before - now) * LOG2)
        totals = jnp.sum(lb[at, :] * shrink + lanes(weights), axis=-1, keepdims=True)
        sums = ab[at, :] * shrink + jnp.dot(
            weights.astype(BF16), kvb[1], preferred_element_type=F32
        )
        level = jnp.broadcast_to(now * LOG2 + jnp.log2(totals), sums.shape)
        return sums / totals, level

    tail = pl.ds(2 * SPAN, 4 * TXT)

    def state_rows(p, slot):
        return pl.ds(pl.multiple_of((p * 4 + slot) * SLOT, SLOT), SLOT)

    def open_phase(p):
        def pair(i, _):
            slots = (3 * i, 1 + i)
            for slot in slots:
                await_q(p, slot)
            for slot in slots:
                open_step(qb[p, slot], state_rows(p, slot))
            return 0

        lax.fori_loop(0, 2, pair, 0)

    def out_copies(p, j, slot, i, r):
        device = along("zl", j, r)
        return (
            remote(
                ob.at[p, j, pl.ds(pl.multiple_of(r * HALF, HALF), HALF), :], orecv.at[p, slot, c],
                os_.at[p, slot, i], or_.at[p, slot, i], device,
            ),
            remote(
                sb.at[p, j, r], srecv.at[p, slot, c], ss.at[p, slot, i], sr.at[p, slot, i], device
            ),
        )

    def last_phase(p):
        def pair(n, _):
            slots = (2 - 2 * n, 3 - 2 * n)
            for slot in slots:
                mixed, level = last_step(qb[p, slot], state_rows(p, slot))
                ob[p, slot] = mixed.astype(BF16)
                for r in range(2):
                    part = level[r * HALF : (r + 1) * HALF]
                    sb[p, slot, r] = jnp.transpose(part)[:8, :]

            @pl.when(n == 0)
            def _():
                for j in (2, 3):
                    for i, r in enumerate((c, other)):
                        for copy in out_copies(p, j, 4 - j, i, r):
                            copy.start()

            @pl.when(n == 1)
            def _():
                for i, r in enumerate((c, other)):
                    for copy in out_copies(p, 1, 3, i, r):
                        copy.start()
                for copy in out_copies(p, 0, 0, 1, other):
                    copy.start()
                at = pl.ds(pl.multiple_of(c * HALF, HALF), HALF)
                pltpu.make_async_copy(
                    ob.at[p, 0, at, :], orecv.at[p, 0, c], or_.at[p, 0, 0]
                ).start()
                pltpu.make_async_copy(sb.at[p, 0, c], srecv.at[p, 0, c], sr.at[p, 0, 0]).start()

            return 0

        lax.fori_loop(0, 2, pair, 0)

    def merge(p):
        for slot in range(4):
            for i, r in enumerate((c, other)):
                landed(orecv.at[p, slot, r], or_.at[p, slot, i])
                landed(srecv.at[p, slot, r], sr.at[p, slot, i])
        for h in range(2):
            found = [srecv[p, slot, h] for slot in range(4)]
            top = jnp.maximum(jnp.maximum(found[0], found[1]), jnp.maximum(found[2], found[3]))
            weight = [jnp.exp2(part - top) for part in found]
            share = 1.0 / sum(weight)
            mixed = jnp.zeros((HALF, HD), F32)
            for slot in range(4):
                row = (weight[slot] * share)[:1]
                column = jnp.transpose(jnp.broadcast_to(row, (HD, HALF)))
                mixed = mixed + column * orecv[p, slot, h].astype(F32)
            heads[p * HALF : (p + 1) * HALF, h * HD : (h + 1) * HD] = mixed.astype(BF16)

    def send_text():
        mixed, level = last_step(tq[...], tail)
        tob[:, :HD] = mixed
        tob[:, HD:] = level
        for j in range(4):
            slot = (4 - j) % 4
            for i, r in enumerate((c, other)):
                src, dst = tob.at[pl.ds(TXT * j, TXT), :], trecv.at[slot, c]
                if j == 0 and i == 0:
                    pltpu.make_async_copy(src, dst, tr.at[0, 0]).start()
                else:
                    send(remote(src, dst, ts.at[slot, i], tr.at[slot, i], along("zl", j, r)))

    def merge_text():
        for slot in range(4):
            for i, r in enumerate((c, other)):
                landed(trecv.at[slot, r], tr.at[slot, i])
        for h in range(2):
            found = [trecv[slot, h] for slot in range(4)]
            top = found[0][:, HD:]
            for part in found[1:]:
                top = jnp.maximum(top, part[:, HD:])
            weight = [jnp.exp2(part[:, HD:] - top) for part in found]
            mixed = sum(w * part[:, :HD] for w, part in zip(weight, found)) / sum(weight)
            theads[:, h * HD : (h + 1) * HD] = mixed.astype(BF16)

    mirror[0].start()
    spread(0, 0)
    mirror[1].start()
    spread(0, 1)

    @pl.when(low_chip)
    def _():
        text_over.start()

    @pl.when(jnp.logical_and(low_chip, me.x > 0))
    def _():
        text_near.start()

    onward(0, 0)
    onward(0, 1)
    for h in range(2):
        mirror[h].wait_recv()
        spread(1, h)
    load_v.wait()
    gathered(0)
    block(0)
    exchange(0)
    onward(1, 0)
    onward(1, 1)

    @pl.when(jnp.logical_not(stays))
    def _():
        text_near.wait_recv()

    load_t.wait()
    for j in range(3):
        part = jnp.dot(trow[...], wt[j], preferred_element_type=F32)
        tqkv[j] = head_norm(part, gt[j : j + 1]) if j < 2 else part.astype(BF16)
    exchange_text()
    gathered(1)
    block(1)
    exchange(1)
    await_kv(0)
    open_phase(0)
    for j in range(4):
        landed(q_text(j), tqr.at[j])
    open_step(tq[...], tail)
    open_phase(1)
    await_kv(1)
    for j in range(4):
        landed(kv_text(j), tkr.at[j])
    last_phase(1)
    send_text()
    last_phase(0)
    merge(1)
    merge_text()
    merge(0)

    for pair in [mirror] + [found for move in moves for found in move]:
        for copy in pair:
            copy.wait_send()

    @pl.when(low_chip)
    def _():
        text_over.wait_send()

    @pl.when(jnp.logical_and(low_chip, me.x > 0))
    def _():
        text_near.wait_send()

    for copy in sends:
        copy.wait_send()
    for p in range(2):
        for slot in range(4):
            for i, r in enumerate((c, other)):
                if (slot, i) != (0, 0):
                    for copy in out_copies(p, (4 - slot) % 4, slot, i, r):
                        copy.wait_send()


def vmem(n):
    return [pl.BlockSpec(memory_space=pltpu.VMEM)] * n


def hbm(n):
    return [pl.BlockSpec(memory_space=pl.ANY)] * n


DMA = pltpu.SemaphoreType.DMA


def mix(xv, xt, mv, mt, gv, gt, wv, wt):
    states = 2 * SPAN + 4 * TXT
    return pl.pallas_call(
        mix_kernel,
        out_shape=(
            jax.ShapeDtypeStruct((ROWS, 2 * HD), BF16),
            jax.ShapeDtypeStruct((TXT, 2 * HD), BF16),
        ),
        in_specs=vmem(6) + hbm(2),
        out_specs=tuple(vmem(2)),
        scratch_shapes=[
            pltpu.VMEM((8, CHUNK, D), BF16),
            pltpu.VMEM((2, TXT, D), BF16),
            pltpu.VMEM((TXT, D), BF16),
            pltpu.VMEM((3, D, 2 * HD), BF16),
            pltpu.VMEM((3, D, HD), BF16),
            pltpu.VMEM((2, 2, 3, HALF, HD), BF16),
            pltpu.VMEM((3, TXT, HD), BF16),
            pltpu.VMEM((2, 4, SLOT, HD), BF16),
            pltpu.VMEM((2, SPAN, HD), BF16),
            pltpu.VMEM((2, SPAN + 4 * TXT, HD), BF16),
            pltpu.VMEM((4 * TXT, HD), BF16),
            pltpu.VMEM((states, HD), F32),
            pltpu.VMEM((states, HD), F32),
            pltpu.VMEM((states, HD), F32),
            pltpu.VMEM((2, 4, SLOT, HD), BF16),
            pltpu.VMEM((2, 4, 2, 8, HALF), F32),
            pltpu.VMEM((4 * TXT, 2 * HD), F32),
            pltpu.VMEM((2, 4, 2, HALF, HD), BF16),
            pltpu.VMEM((2, 4, 2, 8, HALF), F32),
            pltpu.VMEM((4, 2, TXT, 2 * HD), F32),
            DMA((2,)), DMA((8, 2)), DMA((8, 2)), DMA((2,)), DMA,
        ]
        + [DMA((2, 4, 2))] * 4 + [DMA((4,))] * 4 + [DMA((2, 4, 2))] * 4 + [DMA((4, 2))] * 2,
        compiler_params=pltpu.CompilerParams(collective_id=0, has_side_effects=True),
        name="mix",
    )(xv, xt, mv, mt, gv, gt, wv, wt)


def finish_kernel(
    heads, theads, mv, mt, wv_hbm, wt_hbm, video_out, text_out,
    pb, fb, nb, zb, zs, tp, trb, tfin, tall, wv, wt,
    wsem, fs, fr, ns, nr, zsem, zr, tss, trs, bs, br, xs, xr,
):
    me = Place()
    c = me.c
    half_cols = D // 2
    load_v = pltpu.make_async_copy(wv_hbm, wv, wsem.at[0])
    cols = pl.ds(pl.multiple_of(c * half_cols, half_cols), half_cols)
    load_t = pltpu.make_async_copy(wt_hbm.at[:, cols], wt, wsem.at[1])
    load_v.start()
    load_t.start()
    piece_y, piece_zh, half = me.piece()
    mine = me.y * 2 + me.zh
    home = me.zl // 2 == c

    def gatherer(k):
        return me.at(x=k, zl=2 * c + half, y=piece_y, zh=piece_zh)

    def giver(s):
        y, zh = s // 2, s % 2
        side = jnp.where(me.zh == zh, 0, 1)
        return me.at(x=lax.rem(me.y + 4 - y, 4), zl=2 * side + half, y=y, zh=zh)

    own_piece = jnp.logical_and(me.x == 0, jnp.logical_and(me.zl < 2, c == 0))
    column = [me.at(zl=lax.rem(me.zl + d, 4), c=r) for d in range(4) for r in (c, 1 - c)]
    across = [me.at(x=lax.rem(me.x + d, 4)) for d in range(1, 4)]
    up, down = me.group(1, 0), me.group(3, 0)
    arrived = greet(
        [up, down, me.group(0, 1)] + column[1:] + across,
        4 - jnp.where(own_piece, 1, 0),
    )
    barrier = pltpu.get_barrier_semaphore()

    @pl.when(home)
    def _():
        for s in range(8):
            @pl.when(jnp.logical_not(jnp.logical_and(own_piece, s == mine)))
            def _():
                pl.semaphore_signal(barrier, inc=1, device_id=giver(s), device_id_type=MESH)

    load_v.wait()

    def block(p):
        lhs = heads[p * 4 * CHUNK : (p + 1) * 4 * CHUNK, :]
        for q in range(4):
            span = slice(q * (D // 4), (q + 1) * (D // 4))
            found = jnp.dot(lhs, wv[:, span], preferred_element_type=F32).astype(BF16)
            pb[4 * p : 4 * p + 4, :, span] = found.reshape(4, CHUNK, D // 4)

    block(1)
    arrived()

    far_device = me.at(y=lax.rem(me.y + 3 + 2 * c, 4))
    near_slot = 3 - 2 * c
    plain_device = me.at(y=lax.rem(me.y + 1 + 2 * c, 4))
    plain_slot = 1 + 2 * c

    def part_of(h):
        return pl.ds(h * half_cols, half_cols)

    def far_copy(p, h):
        return remote(
            pb.at[4 * p + 2, :, part_of(h)], fb.at[p, :, part_of(h)],
            fs.at[p, h], fr.at[p, h], far_device,
        )

    def plain_copy(p, h):
        return remote(
            pb.at[4 * p + plain_slot, :, part_of(h)], nb.at[p, 0, :, part_of(h)],
            ns.at[p, 0, h], nr.at[p, 0, h], plain_device,
        )

    def sum_copy(p, h):
        return remote(
            pb.at[4 * p + near_slot, :, part_of(h)], nb.at[p, 1, :, part_of(h)],
            ns.at[p, 1, h], nr.at[p, 1, h], far_device,
        )

    def mirror_copy(h):
        return remote(
            zs.at[:, part_of(h)], zb.at[:, part_of(h)], zsem.at[h], zr.at[h], me.group(0, 1)
        )

    def depart(p):
        for h in range(2):
            far_copy(p, h).start()
            plain_copy(p, h).start()

    def relay(p, h):
        far_copy(p, h).wait_recv()
        at = part_of(h)
        total = pb[4 * p + near_slot, :, at].astype(F32) + fb[p, :, at].astype(F32)
        pb[4 * p + near_slot, :, at] = total.astype(BF16)
        sum_copy(p, h).start()

    def collect(p, h):
        plain_copy(p, h).wait_recv()
        sum_copy(p, h).wait_recv()
        at = part_of(h)
        return (
            pb[4 * p, :, at].astype(F32) + nb[p, 0, :, at].astype(F32) + nb[p, 1, :, at].astype(F32)
        )

    depart(1)
    load_t.wait()
    part = jnp.dot(theads[...], wt[...], preferred_element_type=F32).astype(BF16)
    for k in range(4):
        tp[k] = part[:, k * (D // 8) : (k + 1) * (D // 8)]
    text_parts = [
        remote(tp.at[k], trb.at[mine], tss.at[k], trs.at[mine], gatherer(k)) for k in range(4)
    ]
    own_part = pltpu.make_async_copy(tp.at[0], trb.at[mine], trs.at[mine])

    @pl.when(own_piece)
    def _():
        own_part.start()

    @pl.when(jnp.logical_not(own_piece))
    def _():
        text_parts[0].start()

    for text_part in text_parts[1:]:
        text_part.start()
    block(0)
    relay(1, 0)
    relay(1, 1)
    depart(0)
    for h in range(2):
        zs[:, part_of(h)] = collect(1, h).astype(BF16)
        mirror_copy(h).start()

    shares = [
        remote(tfin, tall.at[me.x, half, c], bs.at[i], br.at[half, c], device)
        for i, device in enumerate(column[1:])
    ]

    @pl.when(home)
    def _():
        total = jnp.zeros((TXT, D // 8), F32)
        for s in range(8):
            pltpu.make_async_copy(trb.at[s], trb.at[s], trs.at[s]).wait()
            total = total + trb[s].astype(F32)
        width = D // 8
        at = pl.ds(pl.multiple_of(c * half_cols + me.x * width, width), width)
        tfin[...] = (total * mt[2:3, at].astype(F32)).astype(BF16)
        for share in shares:
            share.start()
        tall[me.x, half, c] = tfin[...]

    relay(0, 0)
    relay(0, 1)
    for b in range(2):
        for r in range(2):
            @pl.when(jnp.logical_not(jnp.logical_and(home, jnp.logical_and(half == b, c == r))))
            def _():
                dst = tall.at[me.x, b, r]
                pltpu.make_async_copy(dst, dst, br.at[b, r]).wait()

    spreads = [
        remote(tall.at[me.x], tall.at[me.x], xs.at[d], xr.at[d], device)
        for d, device in enumerate(across)
    ]
    for copy in spreads:
        copy.start()
    for h in range(2):
        summed = collect(0, h)
        mirror_copy(h).wait_recv()
        at = part_of(h)
        summed = summed + zb[:, at].astype(F32)
        video_out[:, at] = (summed * mv[2:3, at].astype(F32)).astype(BF16)

    for copy in spreads:
        copy.wait_recv()
    for k in range(4):
        for b in range(2):
            for r in range(2):
                at = r * half_cols + k * (D // 8)
                text_out[b * TXT : (b + 1) * TXT, at : at + D // 8] = tall[k, b, r]
    for h in range(2):
        for p in (0, 1):
            far_copy(p, h).wait_send()
            plain_copy(p, h).wait_send()
            sum_copy(p, h).wait_send()
        mirror_copy(h).wait_send()

    @pl.when(jnp.logical_not(own_piece))
    def _():
        text_parts[0].wait_send()

    for copy in text_parts[1:] + spreads:
        copy.wait_send()

    @pl.when(home)
    def _():
        for share in shares:
            share.wait_send()


def finish(heads, theads, mv, mt, wv, wt):
    half_cols = D // 2
    return pl.pallas_call(
        finish_kernel,
        out_shape=(
            jax.ShapeDtypeStruct((CHUNK, D), BF16),
            jax.ShapeDtypeStruct((2 * TXT, D), BF16),
        ),
        in_specs=vmem(4) + hbm(2),
        out_specs=tuple(vmem(2)),
        scratch_shapes=[
            pltpu.VMEM((8, CHUNK, D), BF16),
            pltpu.VMEM((2, CHUNK, D), BF16),
            pltpu.VMEM((2, 2, CHUNK, D), BF16),
            pltpu.VMEM((CHUNK, D), BF16),
            pltpu.VMEM((CHUNK, D), BF16),
            pltpu.VMEM((4, TXT, D // 8), BF16),
            pltpu.VMEM((8, TXT, D // 8), BF16),
            pltpu.VMEM((TXT, D // 8), BF16),
            pltpu.VMEM((4, 2, 2, TXT, D // 8), BF16),
            pltpu.VMEM((2 * HD, D), BF16),
            pltpu.VMEM((2 * HD, half_cols), BF16),
            DMA((2,)), DMA((2, 2)), DMA((2, 2)), DMA((2, 2, 2)), DMA((2, 2, 2)), DMA((2,)), DMA((2,)),
            DMA((4,)), DMA((8,)), DMA((7,)), DMA((2, 2)), DMA((3,)), DMA((3,)),
        ],
        compiler_params=pltpu.CompilerParams(collective_id=1, has_side_effects=True),
        name="finish",
    )(heads, theads, mv, mt, wv, wt)


def settle_kernel(video, text, video_out, text_out):
    video_out[...] = video[...]
    text_out[...] = text[...]


def settle(video, text):
    return pl.pallas_call(
        settle_kernel,
        out_shape=tuple(jax.ShapeDtypeStruct(a.shape, a.dtype) for a in (video, text)),
        in_specs=vmem(2),
        out_specs=tuple(vmem(2)),
        name="settle",
    )(video, text)


def local(
    video_tokens, text_tokens, video_modulation, text_modulation, video_projection,
    text_projection, video_output, text_output, video_gains, text_gains,
):
    heads, theads = mix(
        video_tokens, text_tokens, video_modulation, text_modulation, video_gains, text_gains,
        jnp.transpose(video_projection, (1, 0, 2)), jnp.transpose(text_projection, (1, 0, 2)),
    )
    return settle(
        *finish(heads, theads, video_modulation, text_modulation, video_output, text_output)
    )


def solution(mesh):
    torus = Mesh(mesh.devices.reshape(4, 4, 2, 4, 2), AX)
    placed = (
        P(AX, None),
        P(ULY, None),
        P(),
        P(),
        P(None, None, ULY),
        P(None, None, ULY),
        P(ULY, None),
        P(ULY, None),
        P(),
        P(),
    )
    return jax.shard_map(
        local,
        mesh=torus,
        in_specs=placed,
        out_specs=(P(AX, None), P(ULY, None)),
        check_vma=False,
    )
```
